32 devices in a mesh: dom: 4 (over y, x), fsdp: 8 (over z, core).
Axes of the slice: x: 2, y: 2, z: 4, core: 2. Of those that a mesh axis runs over, the one named last changes fastest.
Arguments:
- inputs: bfloat16 [4, 1024, 4096], P('dom', 'fsdp'), may hold values from -6 to 6
- cotangent: bfloat16 [4, 1024, 8192], P('dom', 'fsdp'), may hold values from -6 to 6
- shared_weight: bfloat16 [4096, 8192], P(None, 'fsdp'), may hold values from -0.09375 to 0.09375
- domain_weight: bfloat16 [4, 4096, 8192], P('dom', None, 'fsdp'), may hold values from 0.099609375 to 1.8984375
- row_counts: int32 [4], P('dom'), may hold values from 65 to 1024, as said below
Outputs:
- shared_grad: float32 [4096, 8192], P('dom', 'fsdp')
- domain_grad: bfloat16 [4, 4096, 8192], P('dom', None, 'fsdp')
- input_grad: bfloat16 [4, 1024, 4096], P('dom', 'fsdp')
The draws below stay inside these ranges and needn't reach their ends.
Inputs may be any that keep to these rules, and one draw needn't show every extreme that they name: `row_counts`: rows of a domain at positions from its count on are padding. Some domain is full in every draw.
All inputs are finite; a program needn't handle non-finite values.
Results may differ from the reference program's by a relative error of at most 0.017.
Values may be sent and summed in bfloat16 or wider, within the bound.
A program may use at most 128 MiB of HBM per device.

```python
import jax
import jax.numpy as jnp
from jax import lax

D = 4096
H = 8192
DOMS = 4
CAP = 1024
N_FSDP = 8


def draw_row_counts(key, part):
    first, second, third = jax.random.split(jax.random.fold_in(key, 7), 3)
    shifts = jax.random.randint(first, (DOMS,), 0, 4)
    base = CAP // jnp.left_shift(jnp.int32(1), shifts.astype(jnp.int32))
    jitter = jax.random.randint(second, (DOMS,), 0, 1 << 30) % (base // 2)
    counts = base - jitter
    fuller = jax.random.randint(third, (), 0, DOMS)
    counts = jnp.where(jnp.arange(DOMS) == fuller, CAP, counts)
    return counts.astype(jnp.int32)


def shard_levels(stream_key, dims, pieces, smallest, top_value):
    gain = 1.0
    for axis_at, shards_of in pieces:
        heights = jax.random.uniform(jax.random.fold_in(jax.random.fold_in(stream_key, 6), axis_at), (shards_of,), jnp.float32, smallest / len(pieces), top_value / len(pieces))
        gain = gain * jnp.repeat(jnp.exp(heights), dims[axis_at] // shards_of).reshape((-1,) + (1,) * (len(dims) - 1 - axis_at))
    return gain


def gaussian(rng, extent, spread, bound, cuts=(), held_as=jnp.bfloat16):
    loudness = shard_levels(rng, extent, cuts, -0.22, 0.18) if cuts else 1.0
    result = jax.random.normal(rng, extent, jnp.float32) * spread * loudness
    return jnp.minimum(jnp.maximum(result, -bound), bound).astype(held_as)


def setup_inputs(seed: int = 0) -> dict:
    keys = jax.random.split(jax.random.key(seed), 6)
    return {
        "inputs": gaussian(keys[0], (DOMS, CAP, D), 1.0, 6.0, ((0, 4), (1, 8))),
        "cotangent": gaussian(keys[1], (DOMS, CAP, H), 1.0, 6.0, ((0, 4), (1, 8))),
        "shared_weight": gaussian(keys[2], (D, H), D ** -0.5, 0.09375, ((1, 8),)),
        "domain_weight": jnp.clip(1.0 + 0.18 * jax.random.normal(keys[3], (DOMS, D, H), jnp.float32), 0.099609375, 1.8984375).astype(jnp.bfloat16),
        "row_counts": draw_row_counts(jax.random.fold_in(keys[5], 71), 0),
    }


def domain_pass(shared_weight, inputs_g, upstream_g, weight_g, count_g):
    effective = (shared_weight.astype(jnp.float32) * weight_g.astype(jnp.float32)).astype(jnp.bfloat16)
    preact = jnp.dot(inputs_g, effective, preferred_element_type=jnp.float32)
    sigma = jax.nn.sigmoid(preact)
    position = jnp.arange(CAP, dtype=jnp.int32)
    live = (position < count_g)[:, None]
    slope = upstream_g.astype(jnp.float32) * sigma * (1.0 + preact * (1.0 - sigma))
    grad_pre = jnp.where(live, slope, jnp.float32(0.0)).astype(jnp.bfloat16)
    scale = lax.rsqrt(count_g.astype(jnp.float32))
    weight_sum = jnp.dot(inputs_g.T, grad_pre, preferred_element_type=jnp.float32) * scale
    shared_term = weight_sum * weight_g.astype(jnp.float32)
    domain_grad = (weight_sum * shared_weight.astype(jnp.float32)).astype(jnp.bfloat16)
    width = H // N_FSDP

    def add_block(total, block):
        start = (block * width).astype(jnp.int32)
        grad_cols = lax.dynamic_slice_in_dim(grad_pre, start, width, 1)
        eff_cols = lax.dynamic_slice_in_dim(effective, start, width, 1)
        partial_sum = jnp.dot(grad_cols, eff_cols.T, preferred_element_type=jnp.float32)
        rounded = lax.optimization_barrier(partial_sum.astype(jnp.bfloat16))
        return (total + rounded.astype(jnp.float32), None)
    total, _ = lax.scan(add_block, jnp.zeros((CAP, D), jnp.float32), jnp.arange(N_FSDP, dtype=jnp.int32))
    return (shared_term, domain_grad, total.astype(jnp.bfloat16))

def reference(inputs, cotangent, shared_weight, domain_weight, row_counts):

    def step(carry, items):
        inputs_g, upstream_g, weight_g, count_g = items
        shared_term, domain_grad, input_grad = domain_pass(shared_weight, inputs_g, upstream_g, weight_g, count_g)
        return (carry + shared_term, (domain_grad, input_grad))
    shared_grad, outputs = lax.scan(step, jnp.zeros((D, H), jnp.float32), (inputs, cotangent, domain_weight, row_counts))
    return (shared_grad, outputs[0], outputs[1])
```

```python
import functools

import jax
import jax.numpy as jnp
from jax import lax
from jax.experimental import pallas as pl
from jax.experimental.pallas import tpu as pltpu
from jax.sharding import PartitionSpec as P

MESH = pl.DeviceIdType.MESH
F32 = jnp.float32
BF16 = jnp.bfloat16


def entry_barrier(axis, me, n):
    barrier = pltpu.get_barrier_semaphore()

    def greet(k, carry):
        pl.semaphore_signal(
            barrier, inc=1, device_id={axis: lax.rem(me + k, n)}, device_id_type=MESH
        )
        return carry

    lax.fori_loop(1, n, greet, 0)
    pl.semaphore_wait(barrier, n - 1)


def first_kernel(
    n, x_ref, g_ref, sw_ref, dw_ref, count_ref, x_out, gp_out, dx_out,
    xs, gs, gp, dx, weff, swb, dwb,
    up_sem, down_sem, side_sem, x_sem, gsend_sem, g_sem, load_sem, own_sem, out_sem,
):
    me = lax.axis_index("fsdp")
    nz = n // 2
    z, c = lax.div(me, 2), lax.rem(me, 2)
    rows, depth = x_ref.shape
    width = sw_ref.shape[1]
    tile = swb.shape[1]

    entry_barrier("fsdp", me, n)

    def slot(buf, chip, core):
        return buf.at[chip, pl.ds(pl.multiple_of(core * rows, rows), rows)]

    def x_copy(src, chip, core, sem, target):
        return pltpu.make_async_remote_copy(
            src_ref=src,
            dst_ref=slot(xs, chip, core),
            send_sem=sem.at[chip],
            recv_sem=x_sem.at[chip * 2 + core],
            device_id={"fsdp": target},
            device_id_type=MESH,
        )

    def g_copy(target):
        cols = pl.ds(pl.multiple_of(target * width, width), width)
        return pltpu.make_async_remote_copy(
            src_ref=g_ref.at[:, cols],
            dst_ref=slot(gs, z, c),
            send_sem=gsend_sem.at[target],
            recv_sem=g_sem.at[me],
            device_id={"fsdp": target},
            device_id_type=MESH,
        )

    up, down, sibling = me + 2, me - 2, z * 2 + (1 - c)

    @pl.when(z + 1 < nz)
    def _():
        x_copy(x_ref, z, c, up_sem, up).start()

    @pl.when(z > 0)
    def _():
        x_copy(x_ref, z, c, down_sem, down).start()

    x_copy(x_ref, z, c, side_sem, sibling).start()

    def send_g(k, carry):
        g_copy(lax.rem(me + k, n)).start()
        return carry

    lax.fori_loop(1, n, send_g, 0)

    own_x = pltpu.make_async_copy(x_ref, slot(xs, z, c), own_sem.at[0])
    own_g = pltpu.make_async_copy(
        g_ref.at[:, pl.ds(pl.multiple_of(me * width, width), width)], slot(gs, z, c), own_sem.at[1]
    )
    own_x.start()
    own_g.start()

    def load(i, b):
        at = pl.ds(pl.multiple_of(i * tile, tile), tile)
        return (
            pltpu.make_async_copy(sw_ref.at[at], swb.at[b], load_sem.at[b, 0]),
            pltpu.make_async_copy(dw_ref.at[at], dwb.at[b], load_sem.at[b, 1]),
        )

    tiles = depth // tile
    for copy in load(0, 0):
        copy.start()

    def make_weff(i, carry):
        b = lax.rem(i, 2)

        @pl.when(i + 1 < tiles)
        def _():
            for copy in load(i + 1, 1 - b):
                copy.start()

        for copy in load(i, b):
            copy.wait()
        at = pl.ds(pl.multiple_of(i * tile, tile), tile)
        weff[at, :] = (swb[b].astype(F32) * dwb[b].astype(F32)).astype(BF16)
        return carry

    lax.fori_loop(0, tiles, make_weff, 0)
    own_x.wait()
    own_g.wait()

    count = count_ref[0]
    wt = min(256, width)
    dt = min(512, depth)

    def out_copies(chip):
        return (
            pltpu.make_async_copy(xs.at[chip], x_out.at[chip], out_sem.at[chip, 0]),
            pltpu.make_async_copy(gp.at[chip], gp_out.at[chip], out_sem.at[chip, 1]),
            pltpu.make_async_copy(dx.at[chip], dx_out.at[chip], out_sem.at[chip, 2]),
        )

    def receive(chip, distance, forward, target, sem):
        @pl.when(distance > 0)
        def _():
            x_copy(slot(xs, chip, c), chip, c, side_sem, sibling).wait_recv()

            @pl.when(forward)
            def _():
                x_copy(slot(xs, chip, c), chip, c, sem, target).start()

            x_copy(slot(xs, chip, c), chip, c, side_sem, sibling).start()

    def compute(chip, distance):
        pltpu.make_async_remote_copy(
            src_ref=slot(xs, chip, 1 - c),
            dst_ref=slot(xs, chip, 1 - c),
            send_sem=side_sem.at[chip],
            recv_sem=x_sem.at[chip * 2 + 1 - c],
            device_id={"fsdp": sibling},
            device_id_type=MESH,
        ).wait_recv()
        copies = out_copies(chip)
        copies[0].start()

        def wait_g(core):
            pltpu.make_async_remote_copy(
                src_ref=slot(gs, chip, core),
                dst_ref=slot(gs, chip, core),
                send_sem=gsend_sem.at[me],
                recv_sem=g_sem.at[chip * 2 + core],
                device_id={"fsdp": sibling},
                device_id_type=MESH,
            ).wait_recv()

        wait_g(1 - c)

        @pl.when(distance > 0)
        def _():
            wait_g(c)

        def pre(i, carry):
            at = pl.ds(pl.multiple_of(i * wt, wt), wt)
            preact = jnp.dot(xs[chip], weff[:, at], preferred_element_type=F32)
            sigma = jax.nn.sigmoid(preact)
            position = chip * (2 * rows) + lax.broadcasted_iota(jnp.int32, preact.shape, 0)
            slope = gs[chip, :, at].astype(F32) * sigma * (1.0 + preact * (1.0 - sigma))
            gp[chip, :, at] = jnp.where(position < count, slope, 0.0).astype(BF16)
            return carry

        lax.fori_loop(0, width // wt, pre, 0)
        copies[1].start()

        def back(i, carry):
            at = pl.ds(pl.multiple_of(i * dt, dt), dt)
            dx[chip, :, at] = lax.dot_general(
                gp[chip], weff[at, :], (((1,), (1,)), ((), ())), preferred_element_type=F32
            ).astype(BF16)
            return carry

        lax.fori_loop(0, depth // dt, back, 0)
        copies[2].start()

    def step(distance, carry):
        below, above = z - distance, z + distance
        has_below = (below >= 0) & (distance > 0)
        has_above = above < nz

        @pl.when(has_below)
        def _():
            receive(below, distance, z + 1 < nz, up, up_sem)

        @pl.when(has_above)
        def _():
            receive(above, distance, z > 0, down, down_sem)

        @pl.when(has_below)
        def _():
            compute(below, distance)

        @pl.when(has_above)
        def _():
            compute(above, distance)

        return carry

    lax.fori_loop(0, nz, step, 0)

    def finish(chip, carry):
        @pl.when((chip <= z) & (z + 1 < nz))
        def _():
            x_copy(slot(xs, chip, c), chip, c, up_sem, up).wait_send()

        @pl.when((chip >= z) & (z > 0))
        def _():
            x_copy(slot(xs, chip, c), chip, c, down_sem, down).wait_send()

        x_copy(slot(xs, chip, c), chip, c, side_sem, sibling).wait_send()
        for copy in out_copies(chip):
            copy.wait()
        return carry

    lax.fori_loop(0, nz, finish, 0)

    def finish_g(k, carry):
        g_copy(lax.rem(me + k, n)).wait_send()
        return carry

    lax.fori_loop(1, n, finish_g, 0)


def forward_and_input_grad(n, x, g, sw, dw, count):
    rows, depth = x.shape
    width = sw.shape[1]
    nz = n // 2
    tile = min(256, depth)
    whole = jax.ShapeDtypeStruct((nz, 2 * rows, depth), BF16)
    cols = jax.ShapeDtypeStruct((nz, 2 * rows, width), BF16)
    any_spec = pl.BlockSpec(memory_space=pl.ANY)
    dma = pltpu.SemaphoreType.DMA
    return pl.pallas_call(
        functools.partial(first_kernel, n),
        out_shape=(whole, cols, whole),
        in_specs=[any_spec] * 4 + [pl.BlockSpec(memory_space=pltpu.SMEM)],
        out_specs=(any_spec,) * 3,
        scratch_shapes=[
            pltpu.VMEM(whole.shape, BF16),
            pltpu.VMEM(cols.shape, BF16),
            pltpu.VMEM(cols.shape, BF16),
            pltpu.VMEM(whole.shape, BF16),
            pltpu.VMEM((depth, width), BF16),
            pltpu.VMEM((2, tile, width), BF16),
            pltpu.VMEM((2, tile, width), BF16),
            dma((nz,)),
            dma((nz,)),
            dma((nz,)),
            dma((n,)),
            dma((n,)),
            dma((n,)),
            dma((2, 2)),
            dma((2,)),
            dma((nz, 3)),
        ],
        compiler_params=pltpu.CompilerParams(
            collective_id=0, has_side_effects=True, vmem_limit_bytes=60 * 1024 * 1024
        ),
        name="gather_and_backprop",
    )(x, g, sw, dw, count)


def solution(mesh):
    n = mesh.shape["fsdp"]

    def body(inputs, cotangent, shared_weight, domain_weight, row_counts):
        live_rows = row_counts[0]
        piece, grad_pre, partial = forward_and_input_grad(
            n, inputs[0], cotangent[0], shared_weight, domain_weight[0], row_counts
        )
        depth = piece.shape[-1]
        piece = piece.reshape(-1, depth)
        grad_pre = grad_pre.reshape(piece.shape[0], -1)
        partial = partial.reshape(-1, depth)
        input_grad = lax.psum_scatter(partial, "fsdp", scatter_dimension=0, tiled=True)
        weight_sum = lax.dot_general(
            piece, grad_pre, (((0,), (0,)), ((), ())), preferred_element_type=F32
        )
        scaled = weight_sum * lax.rsqrt(live_rows.astype(F32))
        shared_grad = lax.psum_scatter(
            (scaled * domain_weight[0].astype(F32)).astype(BF16),
            "dom",
            scatter_dimension=0,
            tiled=True,
        ).astype(F32)
        domain_grad = (scaled * shared_weight.astype(F32)).astype(BF16)
        return (shared_grad, domain_grad[None], input_grad[None])

    return jax.shard_map(
        body,
        mesh=mesh,
        in_specs=(
            P("dom", "fsdp", None),
            P("dom", "fsdp", None),
            P(None, "fsdp"),
            P("dom", None, "fsdp"),
            P("dom"),
        ),
        out_specs=(P("dom", "fsdp"), P("dom", None, "fsdp"), P("dom", "fsdp", None)),
        check_vma=False,
    )
```

```python
import functools

import jax
import jax.numpy as jnp
from jax import lax
from jax.experimental import pallas as pl
from jax.experimental.pallas import tpu as pltpu
from jax.sharding import PartitionSpec as P

MESH = pl.DeviceIdType.MESH
F32 = jnp.float32
BF16 = jnp.bfloat16


def entry_barrier(axis, me, n):
    barrier = pltpu.get_barrier_semaphore()

    def greet(k, carry):
        pl.semaphore_signal(
            barrier, inc=1, device_id={axis: lax.rem(me + k, n)}, device_id_type=MESH
        )
        return carry

    lax.fori_loop(1, n, greet, 0)
    pl.semaphore_wait(barrier, n - 1)


def first_kernel(
    n, x_ref, g_ref, sw_ref, dw_ref, count_ref, x_out, gp_out, dx_out,
    xs, gs, gp, dx, weff, swb, dwb,
    up_sem, down_sem, side_sem, x_sem, gsend_sem, g_sem, load_sem, own_sem, out_sem,
):
    me = lax.axis_index("fsdp")
    nz = n // 2
    z, c = lax.div(me, 2), lax.rem(me, 2)
    rows, depth = x_ref.shape
    width = sw_ref.shape[1]
    tile = swb.shape[1]

    entry_barrier("fsdp", me, n)

    def slot(buf, chip, core):
        return buf.at[chip, pl.ds(pl.multiple_of(core * rows, rows), rows)]

    def x_copy(src, chip, core, sem, target):
        return pltpu.make_async_remote_copy(
            src_ref=src,
            dst_ref=slot(xs, chip, core),
            send_sem=sem.at[chip],
            recv_sem=x_sem.at[chip * 2 + core],
            device_id={"fsdp": target},
            device_id_type=MESH,
        )

    def g_copy(target):
        cols = pl.ds(pl.multiple_of(target * width, width), width)
        return pltpu.make_async_remote_copy(
            src_ref=g_ref.at[:, cols],
            dst_ref=slot(gs, z, c),
            send_sem=gsend_sem.at[target],
            recv_sem=g_sem.at[me],
            device_id={"fsdp": target},
            device_id_type=MESH,
        )

    up, down, sibling = me + 2, me - 2, z * 2 + (1 - c)

    @pl.when(z + 1 < nz)
    def _():
        x_copy(x_ref, z, c, up_sem, up).start()

    @pl.when(z > 0)
    def _():
        x_copy(x_ref, z, c, down_sem, down).start()

    x_copy(x_ref, z, c, side_sem, sibling).start()

    def send_g(k, carry):
        g_copy(lax.rem(me + k, n)).start()
        return carry

    lax.fori_loop(1, n, send_g, 0)

    own_x = pltpu.make_async_copy(x_ref, slot(xs, z, c), own_sem.at[0])
    own_g = pltpu.make_async_copy(
        g_ref.at[:, pl.ds(pl.multiple_of(me * width, width), width)], slot(gs, z, c), own_sem.at[1]
    )
    own_x.start()
    own_g.start()

    def load(i, b):
        at = pl.ds(pl.multiple_of(i * tile, tile), tile)
        return (
            pltpu.make_async_copy(sw_ref.at[at], swb.at[b], load_sem.at[b, 0]),
            pltpu.make_async_copy(dw_ref.at[at], dwb.at[b], load_sem.at[b, 1]),
        )

    tiles = depth // tile
    for copy in load(0, 0):
        copy.start()

    def make_weff(i, carry):
        b = lax.rem(i, 2)

        @pl.when(i + 1 < tiles)
        def _():
            for copy in load(i + 1, 1 - b):
                copy.start()

        for copy in load(i, b):
            copy.wait()
        at = pl.ds(pl.multiple_of(i * tile, tile), tile)
        weff[at, :] = (swb[b].astype(F32) * dwb[b].astype(F32)).astype(BF16)
        return carry

    lax.fori_loop(0, tiles, make_weff, 0)
    own_x.wait()
    own_g.wait()

    count = count_ref[0]
    wt = min(256, width)
    dt = min(512, depth)

    def out_copies(chip):
        return (
            pltpu.make_async_copy(xs.at[chip], x_out.at[chip], out_sem.at[chip, 0]),
            pltpu.make_async_copy(gp.at[chip], gp_out.at[chip], out_sem.at[chip, 1]),
            pltpu.make_async_copy(dx.at[chip], dx_out.at[chip], out_sem.at[chip, 2]),
        )

    def receive(chip, distance, forward, target, sem):
        @pl.when(distance > 0)
        def _():
            x_copy(slot(xs, chip, c), chip, c, side_sem, sibling).wait_recv()

            @pl.when(forward)
            def _():
                x_copy(slot(xs, chip, c), chip, c, sem, target).start()

            x_copy(slot(xs, chip, c), chip, c, side_sem, sibling).start()

    def compute(chip, distance):
        pltpu.make_async_remote_copy(
            src_ref=slot(xs, chip, 1 - c),
            dst_ref=slot(xs, chip, 1 - c),
            send_sem=side_sem.at[chip],
            recv_sem=x_sem.at[chip * 2 + 1 - c],
            device_id={"fsdp": sibling},
            device_id_type=MESH,
        ).wait_recv()
        copies = out_copies(chip)
        copies[0].start()

        def wait_g(core):
            pltpu.make_async_remote_copy(
                src_ref=slot(gs, chip, core),
                dst_ref=slot(gs, chip, core),
                send_sem=gsend_sem.at[me],
                recv_sem=g_sem.at[chip * 2 + core],
                device_id={"fsdp": sibling},
                device_id_type=MESH,
            ).wait_recv()

        wait_g(1 - c)

        @pl.when(distance > 0)
        def _():
            wait_g(c)

        def pre(i, carry):
            at = pl.ds(pl.multiple_of(i * wt, wt), wt)
            preact = jnp.dot(xs[chip], weff[:, at], preferred_element_type=F32)
            sigma = jax.nn.sigmoid(preact)
            position = chip * (2 * rows) + lax.broadcasted_iota(jnp.int32, preact.shape, 0)
            slope = gs[chip, :, at].astype(F32) * sigma * (1.0 + preact * (1.0 - sigma))
            gp[chip, :, at] = jnp.where(position < count, slope, 0.0).astype(BF16)
            return carry

        lax.fori_loop(0, width // wt, pre, 0)
        copies[1].start()

        def back(i, carry):
            at = pl.ds(pl.multiple_of(i * dt, dt), dt)
            dx[chip, :, at] = lax.dot_general(
                gp[chip], weff[at, :], (((1,), (1,)), ((), ())), preferred_element_type=F32
            ).astype(BF16)
            return carry

        lax.fori_loop(0, depth // dt, back, 0)
        copies[2].start()

    def step(distance, carry):
        below, above = z - distance, z + distance
        has_below = (below >= 0) & (distance > 0)
        has_above = above < nz

        @pl.when(has_below)
        def _():
            receive(below, distance, z + 1 < nz, up, up_sem)

        @pl.when(has_above)
        def _():
            receive(above, distance, z > 0, down, down_sem)

        @pl.when(has_below)
        def _():
            compute(below, distance)

        @pl.when(has_above)
        def _():
            compute(above, distance)

        return carry

    lax.fori_loop(0, nz, step, 0)

    def finish(chip, carry):
        @pl.when((chip <= z) & (z + 1 < nz))
        def _():
            x_copy(slot(xs, chip, c), chip, c, up_sem, up).wait_send()

        @pl.when((chip >= z) & (z > 0))
        def _():
            x_copy(slot(xs, chip, c), chip, c, down_sem, down).wait_send()

        x_copy(slot(xs, chip, c), chip, c, side_sem, sibling).wait_send()
        for copy in out_copies(chip):
            copy.wait()
        return carry

    lax.fori_loop(0, nz, finish, 0)

    def finish_g(k, carry):
        g_copy(lax.rem(me + k, n)).wait_send()
        return carry

    lax.fori_loop(1, n, finish_g, 0)


def forward_and_input_grad(n, x, g, sw, dw, count):
    rows, depth = x.shape
    width = sw.shape[1]
    nz = n // 2
    tile = min(256, depth)
    whole = jax.ShapeDtypeStruct((nz, 2 * rows, depth), BF16)
    cols = jax.ShapeDtypeStruct((nz, 2 * rows, width), BF16)
    any_spec = pl.BlockSpec(memory_space=pl.ANY)
    dma = pltpu.SemaphoreType.DMA
    return pl.pallas_call(
        functools.partial(first_kernel, n),
        out_shape=(whole, cols, whole),
        in_specs=[any_spec] * 4 + [pl.BlockSpec(memory_space=pltpu.SMEM)],
        out_specs=(any_spec,) * 3,
        scratch_shapes=[
            pltpu.VMEM(whole.shape, BF16),
            pltpu.VMEM(cols.shape, BF16),
            pltpu.VMEM(cols.shape, BF16),
            pltpu.VMEM(whole.shape, BF16),
            pltpu.VMEM((depth, width), BF16),
            pltpu.VMEM((2, tile, width), BF16),
            pltpu.VMEM((2, tile, width), BF16),
            dma((nz,)),
            dma((nz,)),
            dma((nz,)),
            dma((n,)),
            dma((n,)),
            dma((n,)),
            dma((2, 2)),
            dma((2,)),
            dma((nz, 3)),
        ],
        compiler_params=pltpu.CompilerParams(
            collective_id=0, has_side_effects=True, vmem_limit_bytes=60 * 1024 * 1024
        ),
        name="gather_and_backprop",
    )(x, g, sw, dw, count)


def second_kernel(
    n, nd, x_ref, gp_ref, dx_ref, sw_ref, dw_ref, count_ref, shared_out, dom_out, in_out,
    xv, gv, tb, rb, acc, sib, chain, swb,
    load_sem, acc_sem, sib_send, sib_recv, ch_send, ch_recv, d_send, d_recv, sw_sem, dw_sem, out_sem,
):
    me, dom = lax.axis_index("fsdp"), lax.axis_index("dom")
    nz = n // 2
    z, c = lax.div(me, 2), lax.rem(me, 2)
    sibling = z * 2 + (1 - c)
    bits = nd.bit_length() - 1
    parts = min(2, bits)
    rows = in_out.shape[0]
    width = gv.shape[1]
    half = width // parts
    block = shared_out.shape[0]
    tile = min(256, block)
    pieces = block // tile

    def flip(value, mask):
        for b in range(bits):
            if mask >> b & 1:
                value = value + (1 << b) - (2 << b) * lax.rem(lax.div(value, 1 << b), 2)
        return value

    barrier = pltpu.get_barrier_semaphore()
    for b in range(bits):
        pl.semaphore_signal(
            barrier, inc=1, device_id={"dom": flip(dom, 1 << b)}, device_id_type=MESH
        )
    for near in (lax.rem(me + 2, n), lax.rem(me + n - 2, n), sibling):
        pl.semaphore_signal(barrier, inc=1, device_id={"fsdp": near}, device_id_type=MESH)
    pl.semaphore_wait(barrier, bits + 3)

    load_x = pltpu.make_async_copy(x_ref, xv, load_sem.at[0])
    load_g = pltpu.make_async_copy(gp_ref, gv, load_sem.at[1])
    load_x.start()
    load_g.start()

    order = sorted(range(nd), key=lambda m: (-bin(m).count("1"), m))

    def bit_order(p):
        return [(p + s) % bits for s in range(bits)]

    def sent_at(m, p):
        return next((s for s, b in enumerate(bit_order(p)) if m >> b & 1), bits)

    index = {}
    for p in range(parts):
        for m in range(1, nd):
            s = sent_at(m, p)
            index[p, s, m ^ (1 << bit_order(p)[s])] = len(index)

    def block_rows(m, q):
        return pl.ds(pl.multiple_of(flip(dom, m) * block + q * tile, tile), tile)

    def part(p):
        return pl.ds(p * half, half)

    def piece_rows(q):
        return pl.ds(pl.multiple_of(q * tile, tile), tile)

    def d_copy(m, p, q):
        s = sent_at(m, p)
        bit = 1 << bit_order(p)[s]
        at = index[p, s, m ^ bit]
        return pltpu.make_async_remote_copy(
            src_ref=tb.at[block_rows(m, q), part(p)],
            dst_ref=rb.at[at, piece_rows(q)],
            send_sem=d_send.at[at, q],
            recv_sem=d_recv.at[at, q],
            device_id={"dom": flip(dom, bit)},
            device_id_type=MESH,
        )

    def arrived(m, p, q, steps):
        total = tb[block_rows(m, q), part(p)].astype(F32)
        for s in range(steps):
            at = index[p, s, m]
            pltpu.make_async_remote_copy(
                src_ref=rb.at[at, piece_rows(q)],
                dst_ref=rb.at[at, piece_rows(q)],
                send_sem=d_send.at[at, q],
                recv_sem=d_recv.at[at, q],
                device_id={"dom": flip(dom, 1 << bit_order(p)[s])},
                device_id_type=MESH,
            ).wait_recv()
            total = total + rb[at, piece_rows(q), :].astype(F32)
        return total

    def whole_block(m):
        return pl.ds(pl.multiple_of(flip(dom, m) * block, block), block)

    def sw_load(i):
        return pltpu.make_async_copy(
            sw_ref.at[whole_block(order[i])], swb.at[i % 2], sw_sem.at[i]
        )

    def dw_load(i):
        at = whole_block(order[i])
        return pltpu.make_async_copy(dw_ref.at[at], tb.at[at], dw_sem.at[i])

    def dom_store(i):
        return pltpu.make_async_copy(
            swb.at[i % 2], dom_out.at[whole_block(order[i])], out_sem.at[i]
        )

    sw_load(0).start()
    for i in range(nd):
        dw_load(i).start()

    def own_rows(chip):
        return dx_ref.at[chip, pl.ds(pl.multiple_of(c * rows, rows), rows)]

    def acc_load(chip):
        return pltpu.make_async_copy(own_rows(chip), acc.at[chip], acc_sem.at[chip])

    def sib_copy(chip):
        return pltpu.make_async_remote_copy(
            src_ref=dx_ref.at[chip, pl.ds(pl.multiple_of((1 - c) * rows, rows), rows)],
            dst_ref=sib.at[chip],
            send_sem=sib_send.at[chip],
            recv_sem=sib_recv.at[chip],
            device_id={"fsdp": sibling},
            device_id_type=MESH,
        )

    def chain_copy(slot, chip, target):
        return pltpu.make_async_remote_copy(
            src_ref=acc.at[chip],
            dst_ref=chain.at[slot],
            send_sem=ch_send.at[chip],
            recv_sem=ch_recv.at[slot],
            device_id={"fsdp": target},
            device_id_type=MESH,
        )

    def send_up(chip):
        return chain_copy(chip, chip, lax.rem(me + 2, n))

    def send_down(chip):
        slot = jnp.where(chip == z - 1, nz, chip)
        return chain_copy(slot, chip, lax.rem(me + n - 2, n))

    def start_sib(chip, carry):
        sib_copy(chip).start()
        acc_load(chip).start()
        return carry

    lax.fori_loop(0, nz, start_sib, 0)

    scale = lax.rsqrt(jnp.full((1, 1), count_ref[0], jnp.int32).astype(F32))
    load_x.wait()
    load_g.wait()

    def weight_block(i):
        m = order[i]
        if i + 1 < nd:
            if i >= 1:
                dom_store(i - 1).wait()
            sw_load(i + 1).start()
        sw_load(i).wait()
        dw_load(i).wait()

        def one(q, carry):
            at = block_rows(m, q)
            scaled = scale * lax.dot_general(
                xv[:, at], gv[...], (((0,), (0,)), ((), ())), preferred_element_type=F32
            )
            tb[at, :] = (scaled * tb[at, :].astype(F32)).astype(BF16)
            for p in range(parts):
                if sent_at(m, p) == 0:
                    d_copy(m, p, q).start()
            here = piece_rows(q)
            swb[i % 2, here, :] = (scaled * swb[i % 2, here, :].astype(F32)).astype(BF16)
            return carry

        lax.fori_loop(0, pieces, one, 0)
        dom_store(i).start()

    weight_block(0)

    def pair_sum(k, carry):
        def add(chip):
            acc_load(chip).wait()
            sib_copy(chip).wait_recv()
            acc[chip] = (acc[chip].astype(F32) + sib[chip].astype(F32)).astype(BF16)

        chip = jnp.where(z == 0, nz - 1 - k, k)
        add(chip)

        @pl.when((z == 0) & (chip > z))
        def _():
            send_up(chip).start()

        @pl.when((z == nz - 1) & (chip < z))
        def _():
            send_down(chip).start()

        return carry

    lax.fori_loop(0, nz, pair_sum, 0)

    for i in range(1, nd):
        weight_block(i)

    for s in range(1, bits):
        for m in order:
            for p in range(parts):
                if m and sent_at(m, p) == s:

                    def relay(q, carry, m=m, p=p, s=s):
                        total = arrived(m, p, q, s).astype(BF16)
                        tb[block_rows(m, q), part(p)] = total
                        d_copy(m, p, q).start()
                        return carry

                    lax.fori_loop(0, pieces, relay, 0)

    def hop(t, carry):
        def take(slot, chip):
            pltpu.make_async_remote_copy(
                src_ref=chain.at[slot],
                dst_ref=chain.at[slot],
                send_sem=ch_send.at[chip],
                recv_sem=ch_recv.at[slot],
                device_id={"fsdp": sibling},
                device_id_type=MESH,
            ).wait_recv()
            acc[chip] = (acc[chip].astype(F32) + chain[slot].astype(F32)).astype(BF16)

        rising = nz - 1 - (t - z)
        falling = t - (nz - 1 - z)

        @pl.when((z > 0) & (t >= z))
        def _():
            take(rising, rising)

            @pl.when(rising > z)
            def _():
                send_up(rising).start()

        @pl.when((z < nz - 1) & (falling >= 0))
        def _():
            take(jnp.where(falling == z, nz, falling), falling)

            @pl.when(falling < z)
            def _():
                send_down(falling).start()

        return carry

    lax.fori_loop(1, nz - 1, hop, 0)

    def final(q, carry):
        for p in range(parts):
            shared_out[piece_rows(q), part(p)] = arrived(0, p, q, bits)
        return carry

    lax.fori_loop(0, pieces, final, 0)
    if nz > 1:
        hop(nz - 1, 0)
    in_out[...] = acc[z]

    for i in range(max(0, nd - 2), nd):
        dom_store(i).wait()
    for m in range(1, nd):
        for p in range(parts):

            def drain(q, carry, m=m, p=p):
                d_copy(m, p, q).wait_send()
                return carry

            lax.fori_loop(0, pieces, drain, 0)

    def drain_chain(chip, carry):
        sib_copy(chip).wait_send()

        @pl.when(chip > z)
        def _():
            send_up(chip).wait_send()

        @pl.when(chip < z)
        def _():
            send_down(chip).wait_send()

        return carry

    lax.fori_loop(0, nz, drain_chain, 0)


def weight_grads(n, nd, x, gp, dx, sw, dw, count):
    depth, width = sw.shape
    total = x.shape[0]
    rows = total // n
    nz = n // 2
    bits = nd.bit_length() - 1
    parts = min(2, bits)
    block = depth // nd
    pieces = block // min(256, block)
    buffers = parts * (nd - 1)
    any_spec = pl.BlockSpec(memory_space=pl.ANY)
    vmem_spec = pl.BlockSpec(memory_space=pltpu.VMEM)
    dma = pltpu.SemaphoreType.DMA
    return pl.pallas_call(
        functools.partial(second_kernel, n, nd),
        out_shape=(
            jax.ShapeDtypeStruct((block, width), F32),
            jax.ShapeDtypeStruct((depth, width), BF16),
            jax.ShapeDtypeStruct((rows, depth), BF16),
        ),
        in_specs=[any_spec] * 5 + [pl.BlockSpec(memory_space=pltpu.SMEM)],
        out_specs=(vmem_spec, any_spec, vmem_spec),
        scratch_shapes=[
            pltpu.VMEM((total, depth), BF16),
            pltpu.VMEM((total, width), BF16),
            pltpu.VMEM((depth, width), BF16),
            pltpu.VMEM((buffers, block, width // parts), BF16),
            pltpu.VMEM((nz, rows, depth), BF16),
            pltpu.VMEM((nz, rows, depth), BF16),
            pltpu.VMEM((nz + 1, rows, depth), BF16),
            pltpu.VMEM((2, block, width), BF16),
            dma((2,)),
            dma((nz,)),
            dma((nz,)),
            dma((nz,)),
            dma((nz,)),
            dma((nz + 1,)),
            dma((buffers, pieces)),
            dma((buffers, pieces)),
            dma((nd,)),
            dma((nd,)),
            dma((nd,)),
        ],
        compiler_params=pltpu.CompilerParams(
            collective_id=1, has_side_effects=True, vmem_limit_bytes=62 * 1024 * 1024
        ),
        name="weight_grads",
    )(x, gp, dx, sw, dw, count)


def solution(mesh):
    n, nd = mesh.shape["fsdp"], mesh.shape["dom"]

    def body(inputs, cotangent, shared_weight, domain_weight, row_counts):
        piece, grad_pre, partial = forward_and_input_grad(
            n, inputs[0], cotangent[0], shared_weight, domain_weight[0], row_counts
        )
        depth = piece.shape[-1]
        piece = piece.reshape(-1, depth)
        grad_pre = grad_pre.reshape(piece.shape[0], -1)
        shared_grad, domain_grad, input_grad = weight_grads(
            n, nd, piece, grad_pre, partial, shared_weight, domain_weight[0], row_counts
        )
        return (shared_grad, domain_grad[None], input_grad[None])

    return jax.shard_map(
        body,
        mesh=mesh,
        in_specs=(
            P("dom", "fsdp", None),
            P("dom", "fsdp", None),
            P(None, "fsdp"),
            P("dom", None, "fsdp"),
            P("dom"),
        ),
        out_specs=(P("dom", "fsdp"), P("dom", None, "fsdp"), P("dom", "fsdp", None)),
        check_vma=False,
    )
```

```python
import functools

import jax
import jax.numpy as jnp
from jax import lax
from jax.experimental import pallas as pl
from jax.experimental.pallas import tpu as pltpu
from jax.sharding import PartitionSpec as P

MESH = pl.DeviceIdType.MESH
F32 = jnp.float32
BF16 = jnp.bfloat16


def entry_barrier(axis, me, n):
    barrier = pltpu.get_barrier_semaphore()

    def greet(k, carry):
        pl.semaphore_signal(
            barrier, inc=1, device_id={axis: lax.rem(me + k, n)}, device_id_type=MESH
        )
        return carry

    lax.fori_loop(1, n, greet, 0)
    pl.semaphore_wait(barrier, n - 1)


def first_kernel(
    n, x_ref, g_ref, sw_ref, dw_ref, count_ref, x_out, gp_out, dx_out,
    xs, gs, gp, dx, weff, swb, dwb,
    up_sem, down_sem, side_sem, x_sem, gsend_sem, g_sem, load_sem, own_sem, out_sem,
):
    me = lax.axis_index("fsdp")
    nz = n // 2
    z, c = lax.div(me, 2), lax.rem(me, 2)
    rows, depth = x_ref.shape
    width = sw_ref.shape[1]
    tile = swb.shape[1]

    entry_barrier("fsdp", me, n)

    def slot(buf, chip, core):
        return buf.at[chip, pl.ds(pl.multiple_of(core * rows, rows), rows)]

    def x_copy(src, chip, core, sem, target):
        return pltpu.make_async_remote_copy(
            src_ref=src,
            dst_ref=slot(xs, chip, core),
            send_sem=sem.at[chip],
            recv_sem=x_sem.at[chip * 2 + core],
            device_id={"fsdp": target},
            device_id_type=MESH,
        )

    def g_copy(target):
        cols = pl.ds(pl.multiple_of(target * width, width), width)
        return pltpu.make_async_remote_copy(
            src_ref=g_ref.at[:, cols],
            dst_ref=slot(gs, z, c),
            send_sem=gsend_sem.at[target],
            recv_sem=g_sem.at[me],
            device_id={"fsdp": target},
            device_id_type=MESH,
        )

    up, down, sibling = me + 2, me - 2, z * 2 + (1 - c)

    @pl.when(z + 1 < nz)
    def _():
        x_copy(x_ref, z, c, up_sem, up).start()

    @pl.when(z > 0)
    def _():
        x_copy(x_ref, z, c, down_sem, down).start()

    x_copy(x_ref, z, c, side_sem, sibling).start()

    g_copy(sibling).start()

    def send_g(distance, carry):
        @pl.when(z - distance >= 0)
        def _():
            for core in range(2):
                g_copy((z - distance) * 2 + core).start()

        @pl.when(z + distance < nz)
        def _():
            for core in range(2):
                g_copy((z + distance) * 2 + core).start()

        return carry

    own_x = pltpu.make_async_copy(x_ref, slot(xs, z, c), own_sem.at[0])
    own_g = pltpu.make_async_copy(
        g_ref.at[:, pl.ds(pl.multiple_of(me * width, width), width)], slot(gs, z, c), own_sem.at[1]
    )
    own_x.start()
    own_g.start()

    def load(i, b):
        at = pl.ds(pl.multiple_of(i * tile, tile), tile)
        return (
            pltpu.make_async_copy(sw_ref.at[at], swb.at[b], load_sem.at[b, 0]),
            pltpu.make_async_copy(dw_ref.at[at], dwb.at[b], load_sem.at[b, 1]),
        )

    tiles = depth // tile
    for copy in load(0, 0):
        copy.start()

    def make_weff(i, carry):
        b = lax.rem(i, 2)

        @pl.when(i + 1 < tiles)
        def _():
            for copy in load(i + 1, 1 - b):
                copy.start()

        for copy in load(i, b):
            copy.wait()
        at = pl.ds(pl.multiple_of(i * tile, tile), tile)
        weff[at, :] = (swb[b].astype(F32) * dwb[b].astype(F32)).astype(BF16)
        return carry

    lax.fori_loop(0, tiles, make_weff, 0)
    own_x.wait()
    own_g.wait()

    count = count_ref[0]
    wt = min(256, width)
    dt = min(512, depth)

    def out_copies(chip):
        return (
            pltpu.make_async_copy(xs.at[chip], x_out.at[chip], out_sem.at[chip, 0]),
            pltpu.make_async_copy(gp.at[chip], gp_out.at[chip], out_sem.at[chip, 1]),
            pltpu.make_async_copy(dx.at[chip], dx_out.at[chip], out_sem.at[chip, 2]),
        )

    def receive(chip, distance, forward, target, sem):
        @pl.when(distance > 0)
        def _():
            x_copy(slot(xs, chip, c), chip, c, side_sem, sibling).wait_recv()

            @pl.when(forward)
            def _():
                x_copy(slot(xs, chip, c), chip, c, sem, target).start()

            x_copy(slot(xs, chip, c), chip, c, side_sem, sibling).start()

    def compute(chip, distance):
        pltpu.make_async_remote_copy(
            src_ref=slot(xs, chip, 1 - c),
            dst_ref=slot(xs, chip, 1 - c),
            send_sem=side_sem.at[chip],
            recv_sem=x_sem.at[chip * 2 + 1 - c],
            device_id={"fsdp": sibling},
            device_id_type=MESH,
        ).wait_recv()
        copies = out_copies(chip)
        copies[0].start()

        def wait_g(core):
            pltpu.make_async_remote_copy(
                src_ref=slot(gs, chip, core),
                dst_ref=slot(gs, chip, core),
                send_sem=gsend_sem.at[me],
                recv_sem=g_sem.at[chip * 2 + core],
                device_id={"fsdp": sibling},
                device_id_type=MESH,
            ).wait_recv()

        wait_g(1 - c)

        @pl.when(distance > 0)
        def _():
            wait_g(c)

        def pre(i, carry):
            at = pl.ds(pl.multiple_of(i * wt, wt), wt)
            preact = jnp.dot(xs[chip], weff[:, at], preferred_element_type=F32)
            sigma = jax.nn.sigmoid(preact)
            position = chip * (2 * rows) + lax.broadcasted_iota(jnp.int32, preact.shape, 0)
            slope = gs[chip, :, at].astype(F32) * sigma * (1.0 + preact * (1.0 - sigma))
            gp[chip, :, at] = jnp.where(position < count, slope, 0.0).astype(BF16)
            return carry

        lax.fori_loop(0, width // wt, pre, 0)
        copies[1].start()

        def back(i, carry):
            at = pl.ds(pl.multiple_of(i * dt, dt), dt)
            dx[chip, :, at] = lax.dot_general(
                gp[chip], weff[at, :], (((1,), (1,)), ((), ())), preferred_element_type=F32
            ).astype(BF16)
            return carry

        lax.fori_loop(0, depth // dt, back, 0)
        copies[2].start()

    def step(distance, carry):
        below, above = z - distance, z + distance
        has_below = (below >= 0) & (distance > 0)
        has_above = above < nz

        @pl.when(has_below)
        def _():
            receive(below, distance, z + 1 < nz, up, up_sem)

        @pl.when(has_above)
        def _():
            receive(above, distance, z > 0, down, down_sem)

        @pl.when(distance == 1)
        def _():
            lax.fori_loop(1, nz, send_g, 0)

        @pl.when((below + 1 >= 0) & (distance > 1) & (above - 1 < nz))
        def _():
            compute(above - 1, distance - 1)

        @pl.when(has_below | has_above)
        def _():
            compute(jnp.where(has_below, below, above), distance)

        return carry

    lax.fori_loop(0, nz, step, 0)

    def finish(chip, carry):
        @pl.when((chip <= z) & (z + 1 < nz))
        def _():
            x_copy(slot(xs, chip, c), chip, c, up_sem, up).wait_send()

        @pl.when((chip >= z) & (z > 0))
        def _():
            x_copy(slot(xs, chip, c), chip, c, down_sem, down).wait_send()

        x_copy(slot(xs, chip, c), chip, c, side_sem, sibling).wait_send()
        for copy in out_copies(chip):
            copy.wait()
        return carry

    lax.fori_loop(0, nz, finish, 0)

    def finish_g(k, carry):
        g_copy(lax.rem(me + k, n)).wait_send()
        return carry

    lax.fori_loop(1, n, finish_g, 0)


def forward_and_input_grad(n, x, g, sw, dw, count):
    rows, depth = x.shape
    width = sw.shape[1]
    nz = n // 2
    tile = min(256, depth)
    whole = jax.ShapeDtypeStruct((nz, 2 * rows, depth), BF16)
    cols = jax.ShapeDtypeStruct((nz, 2 * rows, width), BF16)
    any_spec = pl.BlockSpec(memory_space=pl.ANY)
    dma = pltpu.SemaphoreType.DMA
    return pl.pallas_call(
        functools.partial(first_kernel, n),
        out_shape=(whole, cols, whole),
        in_specs=[any_spec] * 4 + [pl.BlockSpec(memory_space=pltpu.SMEM)],
        out_specs=(any_spec,) * 3,
        scratch_shapes=[
            pltpu.VMEM(whole.shape, BF16),
            pltpu.VMEM(cols.shape, BF16),
            pltpu.VMEM(cols.shape, BF16),
            pltpu.VMEM(whole.shape, BF16),
            pltpu.VMEM((depth, width), BF16),
            pltpu.VMEM((2, tile, width), BF16),
            pltpu.VMEM((2, tile, width), BF16),
            dma((nz,)),
            dma((nz,)),
            dma((nz,)),
            dma((n,)),
            dma((n,)),
            dma((n,)),
            dma((2, 2)),
            dma((2,)),
            dma((nz, 3)),
        ],
        compiler_params=pltpu.CompilerParams(
            collective_id=0, has_side_effects=True, vmem_limit_bytes=60 * 1024 * 1024
        ),
        name="gather_and_backprop",
    )(x, g, sw, dw, count)


def second_kernel(
    n, nd, x_ref, gp_ref, dx_ref, sw_ref, dw_ref, count_ref, shared_out, dom_out, in_out,
    xv, gv, tb, rb, acc, sib, chain, swb,
    load_sem, acc_sem, sib_send, sib_recv, ch_send, ch_recv, d_send, d_recv, sw_sem, dw_sem, out_sem,
):
    me, dom = lax.axis_index("fsdp"), lax.axis_index("dom")
    nz = n // 2
    z, c = lax.div(me, 2), lax.rem(me, 2)
    sibling = z * 2 + (1 - c)
    bits = nd.bit_length() - 1
    parts = min(2, bits)
    rows = in_out.shape[0]
    width = gv.shape[1]
    half = width // parts
    block = shared_out.shape[0]
    tile = min(256, block)
    pieces = block // tile

    def flip(value, mask):
        for b in range(bits):
            if mask >> b & 1:
                value = value + (1 << b) - (2 << b) * lax.rem(lax.div(value, 1 << b), 2)
        return value

    barrier = pltpu.get_barrier_semaphore()
    for b in range(bits):
        pl.semaphore_signal(
            barrier, inc=1, device_id={"dom": flip(dom, 1 << b)}, device_id_type=MESH
        )
    for near in (lax.rem(me + 2, n), lax.rem(me + n - 2, n), sibling):
        pl.semaphore_signal(barrier, inc=1, device_id={"fsdp": near}, device_id_type=MESH)
    pl.semaphore_wait(barrier, bits + 3)

    load_x = pltpu.make_async_copy(x_ref, xv, load_sem.at[0])
    load_g = pltpu.make_async_copy(gp_ref, gv, load_sem.at[1])
    load_x.start()
    load_g.start()

    order = sorted(range(nd), key=lambda m: (-bin(m).count("1"), m))

    def bit_order(p):
        return [(p + s) % bits for s in range(bits)]

    def sent_at(m, p):
        return next((s for s, b in enumerate(bit_order(p)) if m >> b & 1), bits)

    index = {}
    for p in range(parts):
        for m in range(1, nd):
            s = sent_at(m, p)
            index[p, s, m ^ (1 << bit_order(p)[s])] = len(index)

    def block_rows(m, q):
        return pl.ds(pl.multiple_of(flip(dom, m) * block + q * tile, tile), tile)

    def part(p):
        return pl.ds(p * half, half)

    def piece_rows(q):
        return pl.ds(pl.multiple_of(q * tile, tile), tile)

    def d_copy(m, p, q):
        s = sent_at(m, p)
        bit = 1 << bit_order(p)[s]
        at = index[p, s, m ^ bit]
        return pltpu.make_async_remote_copy(
            src_ref=tb.at[block_rows(m, q), part(p)],
            dst_ref=rb.at[at, piece_rows(q)],
            send_sem=d_send.at[at, q],
            recv_sem=d_recv.at[at, q],
            device_id={"dom": flip(dom, bit)},
            device_id_type=MESH,
        )

    def arrived(m, p, q, steps):
        total = tb[block_rows(m, q), part(p)].astype(F32)
        for s in range(steps):
            at = index[p, s, m]
            pltpu.make_async_remote_copy(
                src_ref=rb.at[at, piece_rows(q)],
                dst_ref=rb.at[at, piece_rows(q)],
                send_sem=d_send.at[at, q],
                recv_sem=d_recv.at[at, q],
                device_id={"dom": flip(dom, 1 << bit_order(p)[s])},
                device_id_type=MESH,
            ).wait_recv()
            total = total + rb[at, piece_rows(q), :].astype(F32)
        return total

    def whole_block(m):
        return pl.ds(pl.multiple_of(flip(dom, m) * block, block), block)

    def sw_load(i):
        return pltpu.make_async_copy(
            sw_ref.at[whole_block(order[i])], swb.at[i % 2], sw_sem.at[i]
        )

    def dw_load(i):
        at = whole_block(order[i])
        return pltpu.make_async_copy(dw_ref.at[at], tb.at[at], dw_sem.at[i])

    def dom_store(i):
        return pltpu.make_async_copy(
            swb.at[i % 2], dom_out.at[whole_block(order[i])], out_sem.at[i]
        )

    sw_load(0).start()
    for i in range(nd):
        dw_load(i).start()

    def own_rows(chip):
        return dx_ref.at[chip, pl.ds(pl.multiple_of(c * rows, rows), rows)]

    def acc_load(chip):
        return pltpu.make_async_copy(own_rows(chip), acc.at[chip], acc_sem.at[chip])

    def sib_copy(chip):
        return pltpu.make_async_remote_copy(
            src_ref=dx_ref.at[chip, pl.ds(pl.multiple_of((1 - c) * rows, rows), rows)],
            dst_ref=sib.at[chip],
            send_sem=sib_send.at[chip],
            recv_sem=sib_recv.at[chip],
            device_id={"fsdp": sibling},
            device_id_type=MESH,
        )

    def chain_copy(slot, chip, target):
        return pltpu.make_async_remote_copy(
            src_ref=acc.at[chip],
            dst_ref=chain.at[slot],
            send_sem=ch_send.at[chip],
            recv_sem=ch_recv.at[slot],
            device_id={"fsdp": target},
            device_id_type=MESH,
        )

    def send_up(chip):
        return chain_copy(chip, chip, lax.rem(me + 2, n))

    def send_down(chip):
        slot = jnp.where(chip == z - 1, nz, chip)
        return chain_copy(slot, chip, lax.rem(me + n - 2, n))

    def pair_order(k):
        return jnp.where(z == 0, nz - 1 - k, k)

    def start_sib(k, carry):
        chip = pair_order(k)
        sib_copy(chip).start()
        acc_load(chip).start()
        return carry

    lax.fori_loop(0, nz, start_sib, 0)

    scale = lax.rsqrt(jnp.full((1, 1), count_ref[0], jnp.int32).astype(F32))

    def weight_block(i):
        m = order[i]
        if i + 1 < nd:
            if i >= 1:
                dom_store(i - 1).wait()
            sw_load(i + 1).start()
        sw_load(i).wait()
        dw_load(i).wait()

        def one(q, carry):
            at = block_rows(m, q)
            scaled = scale * lax.dot_general(
                xv[:, at], gv[...], (((0,), (0,)), ((), ())), preferred_element_type=F32
            )
            tb[at, :] = (scaled * tb[at, :].astype(F32)).astype(BF16)
            for p in range(parts):
                if sent_at(m, p) == 0:
                    d_copy(m, p, q).start()
            here = piece_rows(q)
            swb[i % 2, here, :] = (scaled * swb[i % 2, here, :].astype(F32)).astype(BF16)
            return carry

        lax.fori_loop(0, pieces, one, 0)
        dom_store(i).start()

    def pair_sum(k, carry):
        def add(chip):
            acc_load(chip).wait()
            sib_copy(chip).wait_recv()
            acc[chip] = (acc[chip].astype(F32) + sib[chip].astype(F32)).astype(BF16)

        chip = pair_order(k)
        add(chip)

        @pl.when((z == 0) & (chip > z))
        def _():
            send_up(chip).start()

        @pl.when((z == nz - 1) & (chip < z))
        def _():
            send_down(chip).start()

        return carry

    pair_sum(0, 0)
    load_x.wait()
    load_g.wait()
    weight_block(0)
    lax.fori_loop(1, nz, pair_sum, 0)

    for i in range(1, nd):
        weight_block(i)

    def hop(t, carry):
        def take(slot, chip):
            pltpu.make_async_remote_copy(
                src_ref=chain.at[slot],
                dst_ref=chain.at[slot],
                send_sem=ch_send.at[chip],
                recv_sem=ch_recv.at[slot],
                device_id={"fsdp": sibling},
                device_id_type=MESH,
            ).wait_recv()
            acc[chip] = (acc[chip].astype(F32) + chain[slot].astype(F32)).astype(BF16)

        rising = nz - 1 - (t - z)
        falling = t - (nz - 1 - z)

        @pl.when((z > 0) & (t >= z))
        def _():
            take(rising, rising)

            @pl.when(rising > z)
            def _():
                send_up(rising).start()

        @pl.when((z < nz - 1) & (falling >= 0))
        def _():
            take(jnp.where(falling == z, nz, falling), falling)

            @pl.when(falling < z)
            def _():
                send_down(falling).start()

        return carry

    if nz > 2:
        hop(1, 0)
    for s in range(1, bits):
        for m in order:
            for p in range(parts):
                if m and sent_at(m, p) == s:

                    def relay(q, carry, m=m, p=p, s=s):
                        total = arrived(m, p, q, s).astype(BF16)
                        tb[block_rows(m, q), part(p)] = total
                        d_copy(m, p, q).start()
                        return carry

                    lax.fori_loop(0, pieces, relay, 0)

    lax.fori_loop(2, nz - 1, hop, 0)

    def final(q, carry):
        for p in range(parts):
            shared_out[piece_rows(q), part(p)] = arrived(0, p, q, bits)
        return carry

    lax.fori_loop(0, pieces, final, 0)
    if nz > 1:
        hop(nz - 1, 0)
    in_out[...] = acc[z]

    for i in range(max(0, nd - 2), nd):
        dom_store(i).wait()
    for m in range(1, nd):
        for p in range(parts):

            def drain(q, carry, m=m, p=p):
                d_copy(m, p, q).wait_send()
                return carry

            lax.fori_loop(0, pieces, drain, 0)

    def drain_chain(chip, carry):
        sib_copy(chip).wait_send()

        @pl.when(chip > z)
        def _():
            send_up(chip).wait_send()

        @pl.when(chip < z)
        def _():
            send_down(chip).wait_send()

        return carry

    lax.fori_loop(0, nz, drain_chain, 0)


def weight_grads(n, nd, x, gp, dx, sw, dw, count):
    depth, width = sw.shape
    total = x.shape[0]
    rows = total // n
    nz = n // 2
    bits = nd.bit_length() - 1
    parts = min(2, bits)
    block = depth // nd
    pieces = block // min(256, block)
    buffers = parts * (nd - 1)
    any_spec = pl.BlockSpec(memory_space=pl.ANY)
    vmem_spec = pl.BlockSpec(memory_space=pltpu.VMEM)
    dma = pltpu.SemaphoreType.DMA
    return pl.pallas_call(
        functools.partial(second_kernel, n, nd),
        out_shape=(
            jax.ShapeDtypeStruct((block, width), F32),
            jax.ShapeDtypeStruct((depth, width), BF16),
            jax.ShapeDtypeStruct((rows, depth), BF16),
        ),
        in_specs=[any_spec] * 5 + [pl.BlockSpec(memory_space=pltpu.SMEM)],
        out_specs=(vmem_spec, any_spec, vmem_spec),
        scratch_shapes=[
            pltpu.VMEM((total, depth), BF16),
            pltpu.VMEM((total, width), BF16),
            pltpu.VMEM((depth, width), BF16),
            pltpu.VMEM((buffers, block, width // parts), BF16),
            pltpu.VMEM((nz, rows, depth), BF16),
            pltpu.VMEM((nz, rows, depth), BF16),
            pltpu.VMEM((nz + 1, rows, depth), BF16),
            pltpu.VMEM((2, block, width), BF16),
            dma((2,)),
            dma((nz,)),
            dma((nz,)),
            dma((nz,)),
            dma((nz,)),
            dma((nz + 1,)),
            dma((buffers, pieces)),
            dma((buffers, pieces)),
            dma((nd,)),
            dma((nd,)),
            dma((nd,)),
        ],
        compiler_params=pltpu.CompilerParams(
            collective_id=1, has_side_effects=True, vmem_limit_bytes=62 * 1024 * 1024
        ),
        name="weight_grads",
    )(x, gp, dx, sw, dw, count)


def solution(mesh):
    n, nd = mesh.shape["fsdp"], mesh.shape["dom"]

    def body(inputs, cotangent, shared_weight, domain_weight, row_counts):
        piece, grad_pre, partial = forward_and_input_grad(
            n, inputs[0], cotangent[0], shared_weight, domain_weight[0], row_counts
        )
        depth = piece.shape[-1]
        piece = piece.reshape(-1, depth)
        grad_pre = grad_pre.reshape(piece.shape[0], -1)
        shared_grad, domain_grad, input_grad = weight_grads(
            n, nd, piece, grad_pre, partial, shared_weight, domain_weight[0], row_counts
        )
        return (shared_grad, domain_grad[None], input_grad[None])

    return jax.shard_map(
        body,
        mesh=mesh,
        in_specs=(
            P("dom", "fsdp", None),
            P("dom", "fsdp", None),
            P(None, "fsdp"),
            P("dom", None, "fsdp"),
            P("dom"),
        ),
        out_specs=(P("dom", "fsdp"), P("dom", None, "fsdp"), P("dom", "fsdp", None)),
        check_vma=False,
    )
```

```python
import functools

import jax
import jax.numpy as jnp
from jax import lax
from jax.experimental import pallas as pl
from jax.experimental.pallas import tpu as pltpu
from jax.sharding import PartitionSpec as P

MESH = pl.DeviceIdType.MESH
F32 = jnp.float32
BF16 = jnp.bfloat16


def entry_barrier(axis, me, n):
    barrier = pltpu.get_barrier_semaphore()

    def greet(k, carry):
        pl.semaphore_signal(
            barrier, inc=1, device_id={axis: lax.rem(me + k, n)}, device_id_type=MESH
        )
        return carry

    lax.fori_loop(1, n, greet, 0)
    pl.semaphore_wait(barrier, n - 1)


def first_kernel(
    n, x_ref, g_ref, sw_ref, dw_ref, count_ref, x_out, gp_out, dx_out,
    xs, gs, gp, dx, weff, swb, dwb,
    up_sem, down_sem, side_sem, x_sem, gsend_sem, g_sem, load_sem, own_sem, out_sem,
):
    me = lax.axis_index("fsdp")
    nz = n // 2
    z, c = lax.div(me, 2), lax.rem(me, 2)
    rows, depth = x_ref.shape
    width = sw_ref.shape[1]
    tile = swb.shape[1]

    entry_barrier("fsdp", me, n)

    def slot(buf, chip, core):
        return buf.at[chip, pl.ds(pl.multiple_of(core * rows, rows), rows)]

    def x_copy(src, chip, core, sem, target):
        return pltpu.make_async_remote_copy(
            src_ref=src,
            dst_ref=slot(xs, chip, core),
            send_sem=sem.at[chip],
            recv_sem=x_sem.at[chip * 2 + core],
            device_id={"fsdp": target},
            device_id_type=MESH,
        )

    def g_copy(target):
        cols = pl.ds(pl.multiple_of(target * width, width), width)
        return pltpu.make_async_remote_copy(
            src_ref=g_ref.at[:, cols],
            dst_ref=slot(gs, z, c),
            send_sem=gsend_sem.at[target],
            recv_sem=g_sem.at[me],
            device_id={"fsdp": target},
            device_id_type=MESH,
        )

    up, down, sibling = me + 2, me - 2, z * 2 + (1 - c)

    @pl.when(z + 1 < nz)
    def _():
        x_copy(x_ref, z, c, up_sem, up).start()

    @pl.when(z > 0)
    def _():
        x_copy(x_ref, z, c, down_sem, down).start()

    x_copy(x_ref, z, c, side_sem, sibling).start()

    g_copy(sibling).start()

    def send_g(distance, carry):
        @pl.when(z - distance >= 0)
        def _():
            for core in range(2):
                g_copy((z - distance) * 2 + core).start()

        @pl.when(z + distance < nz)
        def _():
            for core in range(2):
                g_copy((z + distance) * 2 + core).start()

        return carry

    own_x = pltpu.make_async_copy(x_ref, slot(xs, z, c), own_sem.at[0])
    own_g = pltpu.make_async_copy(
        g_ref.at[:, pl.ds(pl.multiple_of(me * width, width), width)], slot(gs, z, c), own_sem.at[1]
    )
    own_x.start()
    own_g.start()

    def load(i, b):
        at = pl.ds(pl.multiple_of(i * tile, tile), tile)
        return (
            pltpu.make_async_copy(sw_ref.at[at], swb.at[b], load_sem.at[b, 0]),
            pltpu.make_async_copy(dw_ref.at[at], dwb.at[b], load_sem.at[b, 1]),
        )

    tiles = depth // tile
    for copy in load(0, 0):
        copy.start()

    def make_weff(i, carry):
        b = lax.rem(i, 2)

        @pl.when(i + 1 < tiles)
        def _():
            for copy in load(i + 1, 1 - b):
                copy.start()

        for copy in load(i, b):
            copy.wait()
        at = pl.ds(pl.multiple_of(i * tile, tile), tile)
        weff[at, :] = (swb[b].astype(F32) * dwb[b].astype(F32)).astype(BF16)
        return carry

    lax.fori_loop(0, tiles, make_weff, 0)
    own_x.wait()
    own_g.wait()

    count = count_ref[0]
    wt = min(256, width)
    dt = min(512, depth)

    def out_copies(chip):
        return (
            pltpu.make_async_copy(xs.at[chip], x_out.at[chip], out_sem.at[chip, 0]),
            pltpu.make_async_copy(gp.at[chip], gp_out.at[chip], out_sem.at[chip, 1]),
            pltpu.make_async_copy(dx.at[chip], dx_out.at[chip], out_sem.at[chip, 2]),
        )

    def receive(chip, distance, forward, target, sem):
        @pl.when(distance > 0)
        def _():
            x_copy(slot(xs, chip, c), chip, c, side_sem, sibling).wait_recv()

            @pl.when(forward)
            def _():
                x_copy(slot(xs, chip, c), chip, c, sem, target).start()

            x_copy(slot(xs, chip, c), chip, c, side_sem, sibling).start()

    def compute(chip, distance):
        pltpu.make_async_remote_copy(
            src_ref=slot(xs, chip, 1 - c),
            dst_ref=slot(xs, chip, 1 - c),
            send_sem=side_sem.at[chip],
            recv_sem=x_sem.at[chip * 2 + 1 - c],
            device_id={"fsdp": sibling},
            device_id_type=MESH,
        ).wait_recv()
        copies = out_copies(chip)
        copies[0].start()

        def wait_g(core):
            pltpu.make_async_remote_copy(
                src_ref=slot(gs, chip, core),
                dst_ref=slot(gs, chip, core),
                send_sem=gsend_sem.at[me],
                recv_sem=g_sem.at[chip * 2 + core],
                device_id={"fsdp": sibling},
                device_id_type=MESH,
            ).wait_recv()

        wait_g(1 - c)

        @pl.when(distance > 0)
        def _():
            wait_g(c)

        def pre(i, carry):
            at = pl.ds(pl.multiple_of(i * wt, wt), wt)
            preact = jnp.dot(xs[chip], weff[:, at], preferred_element_type=F32)
            sigma = jax.nn.sigmoid(preact)
            position = chip * (2 * rows) + lax.broadcasted_iota(jnp.int32, preact.shape, 0)
            slope = gs[chip, :, at].astype(F32) * sigma * (1.0 + preact * (1.0 - sigma))
            gp[chip, :, at] = jnp.where(position < count, slope, 0.0).astype(BF16)
            return carry

        lax.fori_loop(0, width // wt, pre, 0)
        copies[1].start()

        def back(i, carry):
            at = pl.ds(pl.multiple_of(i * dt, dt), dt)
            dx[chip, :, at] = lax.dot_general(
                gp[chip], weff[at, :], (((1,), (1,)), ((), ())), preferred_element_type=F32
            ).astype(BF16)
            return carry

        lax.fori_loop(0, depth // dt, back, 0)
        copies[2].start()

    lag = jnp.where((z > 0) & (z < nz - 1), 1, 0)

    def step(distance, carry):
        below, above = z - distance, z + distance
        has_below = (below >= 0) & (distance > 0)
        has_above = above < nz

        @pl.when(has_below)
        def _():
            receive(below, distance, z + 1 < nz, up, up_sem)

        @pl.when(has_above)
        def _():
            receive(above, distance, z > 0, down, down_sem)

        @pl.when(distance == 1)
        def _():
            lax.fori_loop(1, nz, send_g, 0)

        late = distance - lag

        @pl.when((late > 0) & (z - late >= 0))
        def _():
            compute(z - late, late)

        @pl.when((late >= 0) & (z + late < nz))
        def _():
            compute(z + late, late)

        return carry

    lax.fori_loop(0, nz + 1, step, 0)

    def finish(chip, carry):
        @pl.when((chip <= z) & (z + 1 < nz))
        def _():
            x_copy(slot(xs, chip, c), chip, c, up_sem, up).wait_send()

        @pl.when((chip >= z) & (z > 0))
        def _():
            x_copy(slot(xs, chip, c), chip, c, down_sem, down).wait_send()

        x_copy(slot(xs, chip, c), chip, c, side_sem, sibling).wait_send()
        for copy in out_copies(chip):
            copy.wait()
        return carry

    lax.fori_loop(0, nz, finish, 0)

    def finish_g(k, carry):
        g_copy(lax.rem(me + k, n)).wait_send()
        return carry

    lax.fori_loop(1, n, finish_g, 0)


def forward_and_input_grad(n, x, g, sw, dw, count):
    rows, depth = x.shape
    width = sw.shape[1]
    nz = n // 2
    tile = min(256, depth)
    whole = jax.ShapeDtypeStruct((nz, 2 * rows, depth), BF16)
    cols = jax.ShapeDtypeStruct((nz, 2 * rows, width), BF16)
    any_spec = pl.BlockSpec(memory_space=pl.ANY)
    dma = pltpu.SemaphoreType.DMA
    return pl.pallas_call(
        functools.partial(first_kernel, n),
        out_shape=(whole, cols, whole),
        in_specs=[any_spec] * 4 + [pl.BlockSpec(memory_space=pltpu.SMEM)],
        out_specs=(any_spec,) * 3,
        scratch_shapes=[
            pltpu.VMEM(whole.shape, BF16),
            pltpu.VMEM(cols.shape, BF16),
            pltpu.VMEM(cols.shape, BF16),
            pltpu.VMEM(whole.shape, BF16),
            pltpu.VMEM((depth, width), BF16),
            pltpu.VMEM((2, tile, width), BF16),
            pltpu.VMEM((2, tile, width), BF16),
            dma((nz,)),
            dma((nz,)),
            dma((nz,)),
            dma((n,)),
            dma((n,)),
            dma((n,)),
            dma((2, 2)),
            dma((2,)),
            dma((nz, 3)),
        ],
        compiler_params=pltpu.CompilerParams(
            collective_id=0, has_side_effects=True, vmem_limit_bytes=60 * 1024 * 1024
        ),
        name="gather_and_backprop",
    )(x, g, sw, dw, count)


def second_kernel(
    n, nd, x_ref, gp_ref, dx_ref, sw_ref, dw_ref, count_ref, shared_out, dom_out, in_out,
    xv, gv, tb, rb, acc, sib, chain, swb,
    load_sem, acc_sem, sib_send, sib_recv, ch_send, ch_recv, d_send, d_recv, sw_sem, dw_sem, out_sem,
):
    me, dom = lax.axis_index("fsdp"), lax.axis_index("dom")
    nz = n // 2
    z, c = lax.div(me, 2), lax.rem(me, 2)
    sibling = z * 2 + (1 - c)
    bits = nd.bit_length() - 1
    parts = min(2, bits)
    rows = in_out.shape[0]
    width = gv.shape[1]
    half = width // parts
    block = shared_out.shape[0]
    tile = min(256, block)
    pieces = block // tile

    def flip(value, mask):
        for b in range(bits):
            if mask >> b & 1:
                value = value + (1 << b) - (2 << b) * lax.rem(lax.div(value, 1 << b), 2)
        return value

    barrier = pltpu.get_barrier_semaphore()
    for b in range(bits):
        pl.semaphore_signal(
            barrier, inc=1, device_id={"dom": flip(dom, 1 << b)}, device_id_type=MESH
        )
    for near in (lax.rem(me + 2, n), lax.rem(me + n - 2, n), sibling):
        pl.semaphore_signal(barrier, inc=1, device_id={"fsdp": near}, device_id_type=MESH)
    pl.semaphore_wait(barrier, bits + 3)

    load_x = pltpu.make_async_copy(x_ref, xv, load_sem.at[0])
    load_g = pltpu.make_async_copy(gp_ref, gv, load_sem.at[1])
    load_x.start()
    load_g.start()

    order = sorted(range(nd), key=lambda m: (-bin(m).count("1"), m))

    def bit_order(p):
        return [(p + s) % bits for s in range(bits)]

    def sent_at(m, p):
        return next((s for s, b in enumerate(bit_order(p)) if m >> b & 1), bits)

    index = {}
    for p in range(parts):
        for m in range(1, nd):
            s = sent_at(m, p)
            index[p, s, m ^ (1 << bit_order(p)[s])] = len(index)

    def block_rows(m, q):
        return pl.ds(pl.multiple_of(flip(dom, m) * block + q * tile, tile), tile)

    def part(p):
        return pl.ds(p * half, half)

    def piece_rows(q):
        return pl.ds(pl.multiple_of(q * tile, tile), tile)

    def d_copy(m, p, q):
        s = sent_at(m, p)
        bit = 1 << bit_order(p)[s]
        at = index[p, s, m ^ bit]
        return pltpu.make_async_remote_copy(
            src_ref=tb.at[block_rows(m, q), part(p)],
            dst_ref=rb.at[at, piece_rows(q)],
            send_sem=d_send.at[at, q],
            recv_sem=d_recv.at[at, q],
            device_id={"dom": flip(dom, bit)},
            device_id_type=MESH,
        )

    def arrived(m, p, q, steps):
        total = tb[block_rows(m, q), part(p)].astype(F32)
        for s in range(steps):
            at = index[p, s, m]
            pltpu.make_async_remote_copy(
                src_ref=rb.at[at, piece_rows(q)],
                dst_ref=rb.at[at, piece_rows(q)],
                send_sem=d_send.at[at, q],
                recv_sem=d_recv.at[at, q],
                device_id={"dom": flip(dom, 1 << bit_order(p)[s])},
                device_id_type=MESH,
            ).wait_recv()
            total = total + rb[at, piece_rows(q), :].astype(F32)
        return total

    def whole_block(m):
        return pl.ds(pl.multiple_of(flip(dom, m) * block, block), block)

    def sw_load(i):
        return pltpu.make_async_copy(
            sw_ref.at[whole_block(order[i])], swb.at[i % 2], sw_sem.at[i]
        )

    def dw_load(i):
        at = whole_block(order[i])
        return pltpu.make_async_copy(dw_ref.at[at], tb.at[at], dw_sem.at[i])

    def dom_store(i):
        return pltpu.make_async_copy(
            swb.at[i % 2], dom_out.at[whole_block(order[i])], out_sem.at[i]
        )

    sw_load(0).start()
    for i in range(nd):
        dw_load(i).start()

    def own_rows(chip):
        return dx_ref.at[chip, pl.ds(pl.multiple_of(c * rows, rows), rows)]

    def acc_load(chip):
        return pltpu.make_async_copy(own_rows(chip), acc.at[chip], acc_sem.at[chip])

    def sib_copy(chip):
        return pltpu.make_async_remote_copy(
            src_ref=dx_ref.at[chip, pl.ds(pl.multiple_of((1 - c) * rows, rows), rows)],
            dst_ref=sib.at[chip],
            send_sem=sib_send.at[chip],
            recv_sem=sib_recv.at[chip],
            device_id={"fsdp": sibling},
            device_id_type=MESH,
        )

    def chain_copy(slot, chip, target):
        return pltpu.make_async_remote_copy(
            src_ref=acc.at[chip],
            dst_ref=chain.at[slot],
            send_sem=ch_send.at[chip],
            recv_sem=ch_recv.at[slot],
            device_id={"fsdp": target},
            device_id_type=MESH,
        )

    def send_up(chip):
        return chain_copy(chip, chip, lax.rem(me + 2, n))

    def send_down(chip):
        slot = jnp.where(chip == z - 1, nz, chip)
        return chain_copy(slot, chip, lax.rem(me + n - 2, n))

    def pair_order(k):
        return jnp.where(z == 0, nz - 1 - k, k)

    def start_sib(k, carry):
        chip = pair_order(k)
        sib_copy(chip).start()
        acc_load(chip).start()
        return carry

    lax.fori_loop(0, nz, start_sib, 0)

    scale = lax.rsqrt(jnp.full((1, 1), count_ref[0], jnp.int32).astype(F32))

    def weight_block(i):
        m = order[i]
        if i + 1 < nd:
            if i >= 1:
                dom_store(i - 1).wait()
            sw_load(i + 1).start()
        sw_load(i).wait()
        dw_load(i).wait()

        def one(q, carry):
            at = block_rows(m, q)
            scaled = scale * lax.dot_general(
                xv[:, at], gv[...], (((0,), (0,)), ((), ())), preferred_element_type=F32
            )
            tb[at, :] = (scaled * tb[at, :].astype(F32)).astype(BF16)
            for p in range(parts):
                if sent_at(m, p) == 0:
                    d_copy(m, p, q).start()
            here = piece_rows(q)
            swb[i % 2, here, :] = (scaled * swb[i % 2, here, :].astype(F32)).astype(BF16)
            return carry

        lax.fori_loop(0, pieces, one, 0)
        dom_store(i).start()

    def pair_sum(k, carry):
        def add(chip):
            acc_load(chip).wait()
            sib_copy(chip).wait_recv()
            acc[chip] = (acc[chip].astype(F32) + sib[chip].astype(F32)).astype(BF16)

        chip = pair_order(k)
        add(chip)

        @pl.when((z == 0) & (chip > z))
        def _():
            send_up(chip).start()

        @pl.when((z == nz - 1) & (chip < z))
        def _():
            send_down(chip).start()

        return carry

    pair_sum(0, 0)
    load_x.wait()
    load_g.wait()
    weight_block(0)
    lax.fori_loop(1, nz, pair_sum, 0)

    for i in range(1, nd):
        weight_block(i)

    def hop(t, carry):
        def take(slot, chip):
            pltpu.make_async_remote_copy(
                src_ref=chain.at[slot],
                dst_ref=chain.at[slot],
                send_sem=ch_send.at[chip],
                recv_sem=ch_recv.at[slot],
                device_id={"fsdp": sibling},
                device_id_type=MESH,
            ).wait_recv()
            acc[chip] = (acc[chip].astype(F32) + chain[slot].astype(F32)).astype(BF16)

        rising = nz - 1 - (t - z)
        falling = t - (nz - 1 - z)

        @pl.when((z > 0) & (t >= z))
        def _():
            take(rising, rising)

            @pl.when(rising > z)
            def _():
                send_up(rising).start()

        @pl.when((z < nz - 1) & (falling >= 0))
        def _():
            take(jnp.where(falling == z, nz, falling), falling)

            @pl.when(falling < z)
            def _():
                send_down(falling).start()

        return carry

    if nz > 2:
        hop(1, 0)
    for s in range(1, bits):
        for m in order:
            for p in range(parts):
                if m and sent_at(m, p) == s:

                    def relay(q, carry, m=m, p=p, s=s):
                        total = arrived(m, p, q, s).astype(BF16)
                        tb[block_rows(m, q), part(p)] = total
                        d_copy(m, p, q).start()
                        return carry

                    lax.fori_loop(0, pieces, relay, 0)

    lax.fori_loop(2, nz - 1, hop, 0)

    def final(q, carry):
        for p in range(parts):
            shared_out[piece_rows(q), part(p)] = arrived(0, p, q, bits)
        return carry

    lax.fori_loop(0, pieces, final, 0)
    if nz > 1:
        hop(nz - 1, 0)
    in_out[...] = acc[z]

    for i in range(max(0, nd - 2), nd):
        dom_store(i).wait()
    for m in range(1, nd):
        for p in range(parts):

            def drain(q, carry, m=m, p=p):
                d_copy(m, p, q).wait_send()
                return carry

            lax.fori_loop(0, pieces, drain, 0)

    def drain_chain(chip, carry):
        sib_copy(chip).wait_send()

        @pl.when(chip > z)
        def _():
            send_up(chip).wait_send()

        @pl.when(chip < z)
        def _():
            send_down(chip).wait_send()

        return carry

    lax.fori_loop(0, nz, drain_chain, 0)


def weight_grads(n, nd, x, gp, dx, sw, dw, count):
    depth, width = sw.shape
    total = x.shape[0]
    rows = total // n
    nz = n // 2
    bits = nd.bit_length() - 1
    parts = min(2, bits)
    block = depth // nd
    pieces = block // min(256, block)
    buffers = parts * (nd - 1)
    any_spec = pl.BlockSpec(memory_space=pl.ANY)
    vmem_spec = pl.BlockSpec(memory_space=pltpu.VMEM)
    dma = pltpu.SemaphoreType.DMA
    return pl.pallas_call(
        functools.partial(second_kernel, n, nd),
        out_shape=(
            jax.ShapeDtypeStruct((block, width), F32),
            jax.ShapeDtypeStruct((depth, width), BF16),
            jax.ShapeDtypeStruct((rows, depth), BF16),
        ),
        in_specs=[any_spec] * 5 + [pl.BlockSpec(memory_space=pltpu.SMEM)],
        out_specs=(vmem_spec, any_spec, vmem_spec),
        scratch_shapes=[
            pltpu.VMEM((total, depth), BF16),
            pltpu.VMEM((total, width), BF16),
            pltpu.VMEM((depth, width), BF16),
            pltpu.VMEM((buffers, block, width // parts), BF16),
            pltpu.VMEM((nz, rows, depth), BF16),
            pltpu.VMEM((nz, rows, depth), BF16),
            pltpu.VMEM((nz + 1, rows, depth), BF16),
            pltpu.VMEM((2, block, width), BF16),
            dma((2,)),
            dma((nz,)),
            dma((nz,)),
            dma((nz,)),
            dma((nz,)),
            dma((nz + 1,)),
            dma((buffers, pieces)),
            dma((buffers, pieces)),
            dma((nd,)),
            dma((nd,)),
            dma((nd,)),
        ],
        compiler_params=pltpu.CompilerParams(
            collective_id=1, has_side_effects=True, vmem_limit_bytes=62 * 1024 * 1024
        ),
        name="weight_grads",
    )(x, gp, dx, sw, dw, count)


def store_kernel(a_ref, b_ref, c_ref, a_out, b_out, c_out):
    a_out[...] = a_ref[...]
    b_out[...] = b_ref[...]
    c_out[...] = c_ref[...]


def store_results(*arrays):
    steps = 8
    specs = tuple(
        pl.BlockSpec((a.shape[0] // steps, a.shape[1]), lambda i: (i, 0)) for a in arrays
    )
    return pl.pallas_call(
        store_kernel,
        grid=(steps,),
        out_shape=tuple(jax.ShapeDtypeStruct(a.shape, a.dtype) for a in arrays),
        in_specs=specs,
        out_specs=specs,
        compiler_params=pltpu.CompilerParams(vmem_limit_bytes=63 * 1024 * 1024),
        name="store_results",
    )(*arrays)


def solution(mesh):
    n, nd = mesh.shape["fsdp"], mesh.shape["dom"]

    def body(inputs, cotangent, shared_weight, domain_weight, row_counts):
        piece, grad_pre, partial = forward_and_input_grad(
            n, inputs[0], cotangent[0], shared_weight, domain_weight[0], row_counts
        )
        depth = piece.shape[-1]
        piece = piece.reshape(-1, depth)
        grad_pre = grad_pre.reshape(piece.shape[0], -1)
        shared_grad, domain_grad, input_grad = weight_grads(
            n, nd, piece, grad_pre, partial, shared_weight, domain_weight[0], row_counts
        )
        shared_grad, domain_grad, input_grad = store_results(
            shared_grad, domain_grad, input_grad
        )
        return (shared_grad, domain_grad[None], input_grad[None])

    return jax.shard_map(
        body,
        mesh=mesh,
        in_specs=(
            P("dom", "fsdp", None),
            P("dom", "fsdp", None),
            P(None, "fsdp"),
            P("dom", None, "fsdp"),
            P("dom"),
        ),
        out_specs=(P("dom", "fsdp"), P("dom", None, "fsdp"), P("dom", "fsdp", None)),
        check_vma=False,
    )
```

```python
import functools

import jax
import jax.numpy as jnp
from jax import lax
from jax.experimental import pallas as pl
from jax.experimental.pallas import tpu as pltpu
from jax.sharding import PartitionSpec as P

MESH = pl.DeviceIdType.MESH
F32 = jnp.float32
BF16 = jnp.bfloat16


def entry_barrier(axis, me, n):
    barrier = pltpu.get_barrier_semaphore()

    def greet(k, carry):
        pl.semaphore_signal(
            barrier, inc=1, device_id={axis: lax.rem(me + k, n)}, device_id_type=MESH
        )
        return carry

    lax.fori_loop(1, n, greet, 0)
    pl.semaphore_wait(barrier, n - 1)


def first_kernel(
    n, x_ref, g_ref, sw_ref, dw_ref, count_ref, x_out, gp_out, dx_out,
    xs, gs, gp, dx, weff, swb, dwb,
    up_sem, down_sem, side_sem, x_sem, gsend_sem, g_sem, load_sem, own_sem, out_sem,
):
    me = lax.axis_index("fsdp")
    nz = n // 2
    z, c = lax.div(me, 2), lax.rem(me, 2)
    rows, depth = x_ref.shape
    width = sw_ref.shape[1]
    tile = swb.shape[1]

    entry_barrier("fsdp", me, n)

    def slot(buf, chip, core):
        return buf.at[chip, pl.ds(pl.multiple_of(core * rows, rows), rows)]

    def x_copy(src, chip, core, sem, target):
        return pltpu.make_async_remote_copy(
            src_ref=src,
            dst_ref=slot(xs, chip, core),
            send_sem=sem.at[chip],
            recv_sem=x_sem.at[chip * 2 + core],
            device_id={"fsdp": target},
            device_id_type=MESH,
        )

    def g_copy(target):
        cols = pl.ds(pl.multiple_of(target * width, width), width)
        return pltpu.make_async_remote_copy(
            src_ref=g_ref.at[:, cols],
            dst_ref=slot(gs, z, c),
            send_sem=gsend_sem.at[target],
            recv_sem=g_sem.at[me],
            device_id={"fsdp": target},
            device_id_type=MESH,
        )

    up, down, sibling = me + 2, me - 2, z * 2 + (1 - c)

    @pl.when(z + 1 < nz)
    def _():
        x_copy(x_ref, z, c, up_sem, up).start()

    @pl.when(z > 0)
    def _():
        x_copy(x_ref, z, c, down_sem, down).start()

    x_copy(x_ref, z, c, side_sem, sibling).start()

    g_copy(sibling).start()

    def send_g(distance, carry):
        @pl.when(z - distance >= 0)
        def _():
            for core in range(2):
                g_copy((z - distance) * 2 + core).start()

        @pl.when(z + distance < nz)
        def _():
            for core in range(2):
                g_copy((z + distance) * 2 + core).start()

        return carry

    own_x = pltpu.make_async_copy(x_ref, slot(xs, z, c), own_sem.at[0])
    own_g = pltpu.make_async_copy(
        g_ref.at[:, pl.ds(pl.multiple_of(me * width, width), width)], slot(gs, z, c), own_sem.at[1]
    )
    own_x.start()
    own_g.start()

    def load(i, b):
        at = pl.ds(pl.multiple_of(i * tile, tile), tile)
        return (
            pltpu.make_async_copy(sw_ref.at[at], swb.at[b], load_sem.at[b, 0]),
            pltpu.make_async_copy(dw_ref.at[at], dwb.at[b], load_sem.at[b, 1]),
        )

    tiles = depth // tile
    for copy in load(0, 0):
        copy.start()

    def make_weff(i, carry):
        b = lax.rem(i, 2)

        @pl.when(i + 1 < tiles)
        def _():
            for copy in load(i + 1, 1 - b):
                copy.start()

        for copy in load(i, b):
            copy.wait()
        at = pl.ds(pl.multiple_of(i * tile, tile), tile)
        weff[at, :] = (swb[b].astype(F32) * dwb[b].astype(F32)).astype(BF16)
        return carry

    lax.fori_loop(0, tiles, make_weff, 0)
    own_x.wait()
    own_g.wait()

    count = count_ref[0]
    wt = min(256, width)
    dt = min(512, depth)

    def out_copies(chip):
        return (
            pltpu.make_async_copy(xs.at[chip], x_out.at[chip], out_sem.at[chip, 0]),
            pltpu.make_async_copy(gp.at[chip], gp_out.at[chip], out_sem.at[chip, 1]),
            pltpu.make_async_copy(dx.at[chip], dx_out.at[chip], out_sem.at[chip, 2]),
        )

    def receive(chip, distance, forward, target, sem):
        @pl.when(distance > 0)
        def _():
            x_copy(slot(xs, chip, c), chip, c, side_sem, sibling).wait_recv()

            @pl.when(forward)
            def _():
                x_copy(slot(xs, chip, c), chip, c, sem, target).start()

            x_copy(slot(xs, chip, c), chip, c, side_sem, sibling).start()

    def compute(chip, distance):
        pltpu.make_async_remote_copy(
            src_ref=slot(xs, chip, 1 - c),
            dst_ref=slot(xs, chip, 1 - c),
            send_sem=side_sem.at[chip],
            recv_sem=x_sem.at[chip * 2 + 1 - c],
            device_id={"fsdp": sibling},
            device_id_type=MESH,
        ).wait_recv()
        copies = out_copies(chip)
        copies[0].start()

        def wait_g(core):
            pltpu.make_async_remote_copy(
                src_ref=slot(gs, chip, core),
                dst_ref=slot(gs, chip, core),
                send_sem=gsend_sem.at[me],
                recv_sem=g_sem.at[chip * 2 + core],
                device_id={"fsdp": sibling},
                device_id_type=MESH,
            ).wait_recv()

        wait_g(1 - c)

        @pl.when(distance > 0)
        def _():
            wait_g(c)

        def pre(i, carry):
            at = pl.ds(pl.multiple_of(i * wt, wt), wt)
            preact = jnp.dot(xs[chip], weff[:, at], preferred_element_type=F32)
            sigma = jax.nn.sigmoid(preact)
            position = chip * (2 * rows) + lax.broadcasted_iota(jnp.int32, preact.shape, 0)
            slope = gs[chip, :, at].astype(F32) * sigma * (1.0 + preact * (1.0 - sigma))
            gp[chip, :, at] = jnp.where(position < count, slope, 0.0).astype(BF16)
            return carry

        lax.fori_loop(0, width // wt, pre, 0)
        copies[1].start()

        def back(i, carry):
            at = pl.ds(pl.multiple_of(i * dt, dt), dt)
            dx[chip, :, at] = lax.dot_general(
                gp[chip], weff[at, :], (((1,), (1,)), ((), ())), preferred_element_type=F32
            ).astype(BF16)
            return carry

        lax.fori_loop(0, depth // dt, back, 0)
        copies[2].start()

    lag = jnp.where((z > 0) & (z < nz - 1), 1, 0)

    def step(distance, carry):
        below, above = z - distance, z + distance
        has_below = (below >= 0) & (distance > 0)
        has_above = above < nz

        @pl.when(has_below)
        def _():
            receive(below, distance, z + 1 < nz, up, up_sem)

        @pl.when(has_above)
        def _():
            receive(above, distance, z > 0, down, down_sem)

        @pl.when(distance == 1)
        def _():
            lax.fori_loop(1, nz, send_g, 0)

        late = distance - lag

        @pl.when((late > 0) & (z - late >= 0))
        def _():
            compute(z - late, late)

        @pl.when((late >= 0) & (z + late < nz))
        def _():
            compute(z + late, late)

        return carry

    lax.fori_loop(0, nz + 1, step, 0)

    def finish(chip, carry):
        @pl.when((chip <= z) & (z + 1 < nz))
        def _():
            x_copy(slot(xs, chip, c), chip, c, up_sem, up).wait_send()

        @pl.when((chip >= z) & (z > 0))
        def _():
            x_copy(slot(xs, chip, c), chip, c, down_sem, down).wait_send()

        x_copy(slot(xs, chip, c), chip, c, side_sem, sibling).wait_send()
        for copy in out_copies(chip):
            copy.wait()
        return carry

    lax.fori_loop(0, nz, finish, 0)

    def finish_g(k, carry):
        g_copy(lax.rem(me + k, n)).wait_send()
        return carry

    lax.fori_loop(1, n, finish_g, 0)


def forward_and_input_grad(n, x, g, sw, dw, count):
    rows, depth = x.shape
    width = sw.shape[1]
    nz = n // 2
    tile = min(256, depth)
    whole = jax.ShapeDtypeStruct((nz, 2 * rows, depth), BF16)
    cols = jax.ShapeDtypeStruct((nz, 2 * rows, width), BF16)
    any_spec = pl.BlockSpec(memory_space=pl.ANY)
    dma = pltpu.SemaphoreType.DMA
    return pl.pallas_call(
        functools.partial(first_kernel, n),
        out_shape=(whole, cols, whole),
        in_specs=[any_spec] * 4 + [pl.BlockSpec(memory_space=pltpu.SMEM)],
        out_specs=(any_spec,) * 3,
        scratch_shapes=[
            pltpu.VMEM(whole.shape, BF16),
            pltpu.VMEM(cols.shape, BF16),
            pltpu.VMEM(cols.shape, BF16),
            pltpu.VMEM(whole.shape, BF16),
            pltpu.VMEM((depth, width), BF16),
            pltpu.VMEM((2, tile, width), BF16),
            pltpu.VMEM((2, tile, width), BF16),
            dma((nz,)),
            dma((nz,)),
            dma((nz,)),
            dma((n,)),
            dma((n,)),
            dma((n,)),
            dma((2, 2)),
            dma((2,)),
            dma((nz, 3)),
        ],
        compiler_params=pltpu.CompilerParams(
            collective_id=0, has_side_effects=True, vmem_limit_bytes=60 * 1024 * 1024
        ),
        name="gather_and_backprop",
    )(x, g, sw, dw, count)


def second_kernel(
    n, nd, x_ref, gp_ref, dx_ref, sw_ref, dw_ref, count_ref, shared_out, dom_out, in_out,
    xv, gv, tb, rb, acc, sib, chain, swb,
    load_sem, acc_sem, sib_send, sib_recv, ch_send, ch_recv, d_send, d_recv, sw_sem, dw_sem, out_sem,
):
    me, dom = lax.axis_index("fsdp"), lax.axis_index("dom")
    nz = n // 2
    z, c = lax.div(me, 2), lax.rem(me, 2)
    sibling = z * 2 + (1 - c)
    bits = nd.bit_length() - 1
    parts = min(2, bits)
    rows = in_out.shape[0]
    width = gv.shape[1]
    half = width // parts
    block = shared_out.shape[0]
    tile = min(256, block)
    pieces = block // tile

    def flip(value, mask):
        for b in range(bits):
            if mask >> b & 1:
                value = value + (1 << b) - (2 << b) * lax.rem(lax.div(value, 1 << b), 2)
        return value

    order = sorted(range(nd), key=lambda m: (-bin(m).count("1"), m))

    def bit_order(p):
        return [(p + s) % bits for s in range(bits)]

    def sent_at(m, p):
        return next((s for s, b in enumerate(bit_order(p)) if m >> b & 1), bits)

    index = {}
    for p in range(parts):
        for m in range(1, nd):
            s = sent_at(m, p)
            index[p, s, m ^ (1 << bit_order(p)[s])] = len(index)

    def block_rows(m, q):
        return pl.ds(pl.multiple_of(flip(dom, m) * block + q * tile, tile), tile)

    def part(p):
        return pl.ds(p * half, half)

    def piece_rows(q):
        return pl.ds(pl.multiple_of(q * tile, tile), tile)

    def d_copy(m, p, q):
        s = sent_at(m, p)
        bit = 1 << bit_order(p)[s]
        at = index[p, s, m ^ bit]
        return pltpu.make_async_remote_copy(
            src_ref=tb.at[block_rows(m, q), part(p)],
            dst_ref=rb.at[at, piece_rows(q)],
            send_sem=d_send.at[at, q],
            recv_sem=d_recv.at[at, q],
            device_id={"dom": flip(dom, bit)},
            device_id_type=MESH,
        )

    def arrived(m, p, q, steps):
        total = tb[block_rows(m, q), part(p)].astype(F32)
        for s in range(steps):
            at = index[p, s, m]
            pltpu.make_async_remote_copy(
                src_ref=rb.at[at, piece_rows(q)],
                dst_ref=rb.at[at, piece_rows(q)],
                send_sem=d_send.at[at, q],
                recv_sem=d_recv.at[at, q],
                device_id={"dom": flip(dom, 1 << bit_order(p)[s])},
                device_id_type=MESH,
            ).wait_recv()
            total = total + rb[at, piece_rows(q), :].astype(F32)
        return total

    def whole_block(m):
        return pl.ds(pl.multiple_of(flip(dom, m) * block, block), block)

    def sw_load(i):
        return pltpu.make_async_copy(
            sw_ref.at[whole_block(order[i])], swb.at[i % 2], sw_sem.at[i]
        )

    def dw_load(i):
        at = whole_block(order[i])
        return pltpu.make_async_copy(dw_ref.at[at], tb.at[at], dw_sem.at[i])

    def dom_store(i):
        return pltpu.make_async_copy(
            swb.at[i % 2], dom_out.at[whole_block(order[i])], out_sem.at[i]
        )

    def x_load(i):
        at = whole_block(order[i])
        return pltpu.make_async_copy(x_ref.at[:, at], xv.at[:, at], load_sem.at[i])

    load_g = pltpu.make_async_copy(gp_ref, gv, load_sem.at[nd])
    load_g.start()
    x_load(0).start()
    sw_load(0).start()
    dw_load(0).start()

    barrier = pltpu.get_barrier_semaphore()
    for b in range(bits):
        pl.semaphore_signal(
            barrier, inc=1, device_id={"dom": flip(dom, 1 << b)}, device_id_type=MESH
        )
    for near in (lax.rem(me + 2, n), lax.rem(me + n - 2, n), sibling):
        pl.semaphore_signal(barrier, inc=1, device_id={"fsdp": near}, device_id_type=MESH)
    pl.semaphore_wait(barrier, bits + 3)

    def own_rows(chip):
        return dx_ref.at[chip, pl.ds(pl.multiple_of(c * rows, rows), rows)]

    def acc_load(chip):
        return pltpu.make_async_copy(own_rows(chip), acc.at[chip], acc_sem.at[chip])

    def sib_copy(chip):
        return pltpu.make_async_remote_copy(
            src_ref=dx_ref.at[chip, pl.ds(pl.multiple_of((1 - c) * rows, rows), rows)],
            dst_ref=sib.at[chip],
            send_sem=sib_send.at[chip],
            recv_sem=sib_recv.at[chip],
            device_id={"fsdp": sibling},
            device_id_type=MESH,
        )

    def chain_copy(slot, chip, target):
        return pltpu.make_async_remote_copy(
            src_ref=acc.at[chip],
            dst_ref=chain.at[slot],
            send_sem=ch_send.at[chip],
            recv_sem=ch_recv.at[slot],
            device_id={"fsdp": target},
            device_id_type=MESH,
        )

    def send_up(chip):
        return chain_copy(chip, chip, lax.rem(me + 2, n))

    def send_down(chip):
        slot = jnp.where(chip == z - 1, nz, chip)
        return chain_copy(slot, chip, lax.rem(me + n - 2, n))

    def pair_order(k):
        return jnp.where(z == 0, nz - 1 - k, k)

    def start_sib(k, carry):
        chip = pair_order(k)
        sib_copy(chip).start()
        acc_load(chip).start()
        return carry

    lax.fori_loop(0, nz, start_sib, 0)

    scale = lax.rsqrt(jnp.full((1, 1), count_ref[0], jnp.int32).astype(F32))

    def weight_block(i):
        m = order[i]
        if i + 1 < nd:
            if i >= 1:
                dom_store(i - 1).wait()
            sw_load(i + 1).start()
        sw_load(i).wait()
        dw_load(i).wait()
        x_load(i).wait()

        def one(q, carry):
            at = block_rows(m, q)
            scaled = scale * lax.dot_general(
                xv[:, at], gv[...], (((0,), (0,)), ((), ())), preferred_element_type=F32
            )
            tb[at, :] = (scaled * tb[at, :].astype(F32)).astype(BF16)
            for p in range(parts):
                if sent_at(m, p) == 0:
                    d_copy(m, p, q).start()
            here = piece_rows(q)
            swb[i % 2, here, :] = (scaled * swb[i % 2, here, :].astype(F32)).astype(BF16)
            return carry

        lax.fori_loop(0, pieces, one, 0)
        dom_store(i).start()

    def pair_sum(k, carry):
        def add(chip):
            acc_load(chip).wait()
            sib_copy(chip).wait_recv()
            acc[chip] = (acc[chip].astype(F32) + sib[chip].astype(F32)).astype(BF16)

        chip = pair_order(k)
        add(chip)

        @pl.when((z == 0) & (chip > z))
        def _():
            send_up(chip).start()

        @pl.when((z == nz - 1) & (chip < z))
        def _():
            send_down(chip).start()

        return carry

    for i in range(1, nd):
        x_load(i).start()
        dw_load(i).start()
    pair_sum(0, 0)
    load_g.wait()
    weight_block(0)
    lax.fori_loop(1, nz, pair_sum, 0)

    for i in range(1, nd):
        weight_block(i)

    def hop(t, carry):
        def take(slot, chip):
            pltpu.make_async_remote_copy(
                src_ref=chain.at[slot],
                dst_ref=chain.at[slot],
                send_sem=ch_send.at[chip],
                recv_sem=ch_recv.at[slot],
                device_id={"fsdp": sibling},
                device_id_type=MESH,
            ).wait_recv()
            acc[chip] = (acc[chip].astype(F32) + chain[slot].astype(F32)).astype(BF16)

        rising = nz - 1 - (t - z)
        falling = t - (nz - 1 - z)

        @pl.when((z > 0) & (t >= z))
        def _():
            take(rising, rising)

            @pl.when(rising > z)
            def _():
                send_up(rising).start()

        @pl.when((z < nz - 1) & (falling >= 0))
        def _():
            take(jnp.where(falling == z, nz, falling), falling)

            @pl.when(falling < z)
            def _():
                send_down(falling).start()

        return carry

    if nz > 2:
        hop(1, 0)
    for s in range(1, bits):
        for m in order:
            for p in range(parts):
                if m and sent_at(m, p) == s:

                    def relay(q, carry, m=m, p=p, s=s):
                        total = arrived(m, p, q, s).astype(BF16)
                        tb[block_rows(m, q), part(p)] = total
                        d_copy(m, p, q).start()
                        return carry

                    lax.fori_loop(0, pieces, relay, 0)

    lax.fori_loop(2, nz - 1, hop, 0)

    def final(q, carry):
        for p in range(parts):
            shared_out[piece_rows(q), part(p)] = arrived(0, p, q, bits)
        return carry

    lax.fori_loop(0, pieces, final, 0)
    if nz > 1:
        hop(nz - 1, 0)
    in_out[...] = acc[z]

    for i in range(max(0, nd - 2), nd):
        dom_store(i).wait()
    for m in range(1, nd):
        for p in range(parts):

            def drain(q, carry, m=m, p=p):
                d_copy(m, p, q).wait_send()
                return carry

            lax.fori_loop(0, pieces, drain, 0)

    def drain_chain(chip, carry):
        sib_copy(chip).wait_send()

        @pl.when(chip > z)
        def _():
            send_up(chip).wait_send()

        @pl.when(chip < z)
        def _():
            send_down(chip).wait_send()

        return carry

    lax.fori_loop(0, nz, drain_chain, 0)


def weight_grads(n, nd, x, gp, dx, sw, dw, count):
    depth, width = sw.shape
    total = x.shape[0]
    rows = total // n
    nz = n // 2
    bits = nd.bit_length() - 1
    parts = min(2, bits)
    block = depth // nd
    pieces = block // min(256, block)
    buffers = parts * (nd - 1)
    any_spec = pl.BlockSpec(memory_space=pl.ANY)
    vmem_spec = pl.BlockSpec(memory_space=pltpu.VMEM)
    dma = pltpu.SemaphoreType.DMA
    return pl.pallas_call(
        functools.partial(second_kernel, n, nd),
        out_shape=(
            jax.ShapeDtypeStruct((block, width), F32),
            jax.ShapeDtypeStruct((depth, width), BF16),
            jax.ShapeDtypeStruct((rows, depth), BF16),
        ),
        in_specs=[any_spec] * 5 + [pl.BlockSpec(memory_space=pltpu.SMEM)],
        out_specs=(vmem_spec, any_spec, vmem_spec),
        scratch_shapes=[
            pltpu.VMEM((total, depth), BF16),
            pltpu.VMEM((total, width), BF16),
            pltpu.VMEM((depth, width), BF16),
            pltpu.VMEM((buffers, block, width // parts), BF16),
            pltpu.VMEM((nz, rows, depth), BF16),
            pltpu.VMEM((nz, rows, depth), BF16),
            pltpu.VMEM((nz + 1, rows, depth), BF16),
            pltpu.VMEM((2, block, width), BF16),
            dma((nd + 1,)),
            dma((nz,)),
            dma((nz,)),
            dma((nz,)),
            dma((nz,)),
            dma((nz + 1,)),
            dma((buffers, pieces)),
            dma((buffers, pieces)),
            dma((nd,)),
            dma((nd,)),
            dma((nd,)),
        ],
        compiler_params=pltpu.CompilerParams(
            collective_id=1, has_side_effects=True, vmem_limit_bytes=62 * 1024 * 1024
        ),
        name="weight_grads",
    )(x, gp, dx, sw, dw, count)


def store_kernel(a_ref, b_ref, c_ref, a_out, b_out, c_out):
    a_out[...] = a_ref[...]
    b_out[...] = b_ref[...]
    c_out[...] = c_ref[...]


def store_results(*arrays):
    steps = 8
    specs = tuple(
        pl.BlockSpec((a.shape[0] // steps, a.shape[1]), lambda i: (i, 0)) for a in arrays
    )
    return pl.pallas_call(
        store_kernel,
        grid=(steps,),
        out_shape=tuple(jax.ShapeDtypeStruct(a.shape, a.dtype) for a in arrays),
        in_specs=specs,
        out_specs=specs,
        compiler_params=pltpu.CompilerParams(vmem_limit_bytes=63 * 1024 * 1024),
        name="store_results",
    )(*arrays)


def solution(mesh):
    n, nd = mesh.shape["fsdp"], mesh.shape["dom"]

    def body(inputs, cotangent, shared_weight, domain_weight, row_counts):
        piece, grad_pre, partial = forward_and_input_grad(
            n, inputs[0], cotangent[0], shared_weight, domain_weight[0], row_counts
        )
        depth = piece.shape[-1]
        piece = piece.reshape(-1, depth)
        grad_pre = grad_pre.reshape(piece.shape[0], -1)
        shared_grad, domain_grad, input_grad = weight_grads(
            n, nd, piece, grad_pre, partial, shared_weight, domain_weight[0], row_counts
        )
        shared_grad, domain_grad, input_grad = store_results(
            shared_grad, domain_grad, input_grad
        )
        return (shared_grad, domain_grad[None], input_grad[None])

    return jax.shard_map(
        body,
        mesh=mesh,
        in_specs=(
            P("dom", "fsdp", None),
            P("dom", "fsdp", None),
            P(None, "fsdp"),
            P("dom", None, "fsdp"),
            P("dom"),
        ),
        out_specs=(P("dom", "fsdp"), P("dom", None, "fsdp"), P("dom", "fsdp", None)),
        check_vma=False,
    )
```
